256 devices in a mesh: gx: 4 (over y), gy: 8 (over x, core), gz: 8 (over z).
Axes of the slice: x: 4, y: 4, z: 8, core: 2. Of those that a mesh axis runs over, the one named last changes fastest.
Arguments:
- source: float32 [64, 128, 1024], P('gx', 'gy', 'gz'), may hold values from -5 to 5
- conductance: float32 [64, 128, 1024], P('gx', 'gy', 'gz'), may hold values from 0.2 to 2
- pressure_start: float32 [64, 128, 1024], P('gx', 'gy', 'gz'), may hold values from -6 to 6
Outputs:
- pressure: float32 [64, 128, 1024], P('gx', 'gy', 'gz')
- residual: float32 [64, 128, 1024], P('gx', 'gy', 'gz')
The draws below stay inside these ranges and needn't reach their ends.
All inputs are finite; a program needn't handle non-finite values.
Results may differ from the reference program's by a relative error of at most 0.0003.
Values sent between devices are 32-bit elements; how exact they have to be, the bound alone decides.
A program may use at most 384 MiB of HBM per device.

```python
import math
import jax
import jax.numpy as jnp

LEVELS = 3
DEG = 3
COARSE_ITERS = 12
NX = 64
NY = 128
NZ = 1024


def draw_source(key, part):
    first = jax.random.fold_in(key, 0)
    return jnp.clip(jax.random.normal(first, (NX, NY, NZ), jnp.float32), -5.0, 5.0)


def block_scale(stream_key, extent, cuts, low, largest):
    level = 1.0
    for dim, parts in cuts:
        draws = jax.random.uniform(jax.random.fold_in(jax.random.fold_in(stream_key, 6), dim), (parts,), jnp.float32, low / len(cuts), largest / len(cuts))
        level = level * jnp.repeat(jnp.exp(draws), extent[dim] // parts).reshape((-1,) + (1,) * (len(extent) - 1 - dim))
    return level


def normal_values(key, dims, width, most, cuts=(), kind=jnp.bfloat16):
    gain = block_scale(key, dims, cuts, -0.22, 0.18) if cuts else 1.0
    values = jax.random.normal(key, dims, jnp.float32) * width * gain
    return jnp.minimum(jnp.maximum(values, -most), most).astype(kind)


def setup_inputs(seed: int = 0) -> dict:
    key_of = jax.random.split(jax.random.key(seed), 4)
    return {
        "source": draw_source(jax.random.fold_in(key_of[3], 71), 0),
        "conductance": jnp.clip(jnp.exp(math.log(2.0) - 2.3025851 * jax.random.uniform(key_of[1], (NX, NY, NZ), jnp.float32) ** block_scale(key_of[1], (NX, NY, NZ), ((0, 4), (1, 8), (2, 8)), -0.2, 0.2)), 0.2, 2.0),
        "pressure_start": normal_values(key_of[2], (NX, NY, NZ), 1.0, 6.0, ((0, 4), (1, 8), (2, 8)), jnp.float32),
    }


SHIFT = 0.001
UPPER_BOUND = 2.0
SMOOTH_FLOOR = 0.5
COARSE_FLOOR = 0.05


def chebyshev_weights(number, floor_value):
    centre = 0.5 * (UPPER_BOUND + floor_value)
    half_width = 0.5 * (UPPER_BOUND - floor_value)
    ratio = centre / half_width
    factor = 1.0 / ratio
    weights = [(0.0, 1.0 / centre)]
    for _ in range(1, number):
        factor_next = 1.0 / (2.0 * ratio - factor)
        weights.append((factor_next * factor, 2.0 * factor_next / half_width))
        factor = factor_next
    return weights


def operate_global(field, conduct):
    total = SHIFT * field
    for axis_id in range(3):
        for offset in (1, -1):
            face = 0.5 * (conduct + jnp.roll(conduct, -offset, axis_id))
            total = total + face * (field - jnp.roll(field, -offset, axis_id))
    return total


def diagonal_global(conduct):
    total = jnp.full_like(conduct, SHIFT)
    for axis_id in range(3):
        for offset in (1, -1):
            total = total + 0.5 * (conduct + jnp.roll(conduct, -offset, axis_id))
    return total


def smooth_global(field, source, conduct, inverse, weights):
    change = jnp.zeros_like(field)
    for carry, weight in weights:
        resid = source - operate_global(field, conduct)
        change = carry * change + weight * inverse * resid
        field = field + change
    return field


def restrict(field):
    extent_x, extent_y, extent_z = field.shape
    return field.reshape(extent_x // 2, 2, extent_y // 2, 2, extent_z // 2, 2).mean(axis=(1, 3, 5))


def prolong(field):
    extent_x, extent_y, extent_z = field.shape
    spread = jnp.broadcast_to(field[:, None, :, None, :, None], (extent_x, 2, extent_y, 2, extent_z, 2))
    return spread.reshape(2 * extent_x, 2 * extent_y, 2 * extent_z)


def coarse_solve(source, conduct):
    inverse = 1.0 / diagonal_global(conduct)
    weights = chebyshev_weights(COARSE_ITERS, COARSE_FLOOR)
    return smooth_global(jnp.zeros_like(source), source, conduct, inverse, weights)


def cycle_global(level, source, conduct, start):
    inverse = 1.0 / diagonal_global(conduct)
    weights = chebyshev_weights(DEG, SMOOTH_FLOOR)
    field = smooth_global(start, source, conduct, inverse, weights)
    resid = source - operate_global(field, conduct)
    coarse_source = restrict(resid)
    coarse_conduct = 0.25 * restrict(conduct)
    if level + 1 == LEVELS:
        correction = coarse_solve(coarse_source, coarse_conduct)
    else:
        correction = cycle_global(level + 1, coarse_source, coarse_conduct, jnp.zeros_like(coarse_source))
    field = field + prolong(correction)
    return smooth_global(field, source, conduct, inverse, weights)


def reference(source, conductance, pressure_start):
    pressure = cycle_global(0, source, conductance, pressure_start)
    residual = source - operate_global(pressure, conductance)
    return pressure, residual
```

```python
import functools
import jax
import jax.numpy as jnp
from jax import lax
from jax.experimental import pallas as pl
from jax.experimental.pallas import tpu as pltpu
from jax.sharding import PartitionSpec as P

DEG = 3
COARSE_ITERS = 12
SHIFT = 0.001
UPPER_BOUND = 2.0
SMOOTH_FLOOR = 0.5
COARSE_FLOOR = 0.05

MESH = pl.DeviceIdType.MESH
AXES = ("gx", "gy", "gz")
COUNT = (4, 8, 8)
F32 = jnp.float32
SIGN = (1, -1)

NEAR = [
    (a, b, c)
    for c in (-1, 0, 1)
    for a in (-1, 0, 1)
    for b in (-1, 0, 1)
    if (a, b, c) != (0, 0, 0)
]
NEAR.sort(key=lambda o: -sum(map(abs, o)))
PLANE = [(a, b, 0) for a in range(4) for b in range(8) if (a, b) != (0, 0)]
RING = [(0, 0, c) for c in range(1, 8)]


def chebyshev_weights(number, floor_value):
    centre = 0.5 * (UPPER_BOUND + floor_value)
    half_width = 0.5 * (UPPER_BOUND - floor_value)
    ratio = centre / half_width
    factor = 1.0 / ratio
    weights = [(0.0, 1.0 / centre)]
    for _ in range(1, number):
        factor_next = 1.0 / (2.0 * ratio - factor)
        weights.append((factor_next * factor, 2.0 * factor_next / half_width))
        factor = factor_next
    return weights


def peer(offset):
    return tuple(
        lax.rem(lax.axis_index(axis) + (step + count), count)
        for axis, step, count in zip(AXES, offset, COUNT)
    )


def iota(shape, dim):
    return lax.broadcasted_iota(jnp.int32, shape, dim)


def roll(value, shift, dim):
    size = value.shape[dim]
    return pltpu.roll(value, shift % size, dim)


def dot(left, right):
    return jnp.dot(left, right, precision=lax.Precision.HIGHEST, preferred_element_type=F32)


def ones_where(mask, scale=1.0):
    return jnp.where(mask, F32(scale), F32(0.0))


def send(src, dst, ssem, rsem, offset):
    pltpu.make_async_remote_copy(
        src_ref=src, dst_ref=dst, send_sem=ssem, recv_sem=rsem,
        device_id=peer(offset), device_id_type=MESH,
    ).start()


def wait_bytes(ref, sem):
    pltpu.make_async_copy(ref, ref, sem).wait()


def pack_fine(ext, count, py, pz):
    sub = iota((8, 128), 0)
    lane = iota((8, 128), 1)
    for a in range(count):
        for group in range(4):
            for r in range(2):
                first = 4 + 4 * group + r
                slot = 2 * group + r
                py[0, a, slot] = jnp.where(
                    sub >= 4, ext[a, first, 8:16, 0:128], roll(ext[a, first + 2, 8:16, 0:128], 4, 0)
                )
                py[1, a, slot] = jnp.where(
                    sub < 4, ext[a, first, 0:8, 0:128], roll(ext[a, first + 2, 0:8, 0:128], 4, 0)
                )
        for tile in range(2):
            acc = jnp.zeros((8, 128), F32)
            for x in range(16):
                row = ext[a, 4 + x, 8 * tile : 8 * tile + 8, 0:128]
                acc = jnp.where(lane // 8 == x, roll(row, 8 * x + 4, 1), acc)
            pz[a, tile] = acc


def send_fine(ext, py, pz, recv, ssem, rsem):
    ry, rz, rxy, rxz, ryz, rxyz = recv
    for offset in NEAR:
        dx, dy, dz = offset
        xi, yi, zi = (0 if d == 1 else 1 for d in offset)
        kind = (dx != 0, dy != 0, dz != 0)
        tile = 1 if dy == 1 else 0
        planes = pl.ds(6, 2) if dx == 1 else pl.ds(0, 2)
        if kind == (True, False, False):
            src = ext.at[:, pl.ds(16 if dx == 1 else 4, 4), pl.ds(0, 16), pl.ds(0, 128)]
            dst = ext.at[:, pl.ds(0 if dx == 1 else 20, 4), pl.ds(0, 16), pl.ds(0, 128)]
            which = 0
        elif kind == (False, True, False):
            src, dst, which = py.at[yi], ry.at[yi], 1
        elif kind == (False, False, True):
            src, dst, which = pz, rz.at[zi], 2
        elif kind == (True, True, False):
            src, dst, which = py.at[yi, :, planes], rxy.at[xi, yi], 3
        elif kind == (True, False, True):
            src, dst, which = pz, rxz.at[xi, zi], 4
        elif kind == (False, True, True):
            src, dst, which = pz.at[:, tile], ryz.at[yi, zi], 5
        else:
            src, dst, which = pz.at[:, tile], rxyz.at[xi, yi, zi], 6
        send(src, dst, ssem.at[which], rsem.at[which], offset)


def wait_fine(py, recv, sem):
    refs = (recv[0].at[:, :, pl.ds(0, 8)],) + recv
    for which in range(7):
        wait_bytes(refs[which], sem.at[which])


def unpack_fine(ext, count, recv):
    ry, rz, rxy, rxz, ryz, rxyz = recv
    sub = iota((8, 128), 0)
    lane = iota((8, 128), 1)
    low = sub < 4
    zleft = lane % 8 < 4

    def place(a, first, left, right):
        ext[a, first, 16:24, 0:128] = jnp.where(low, right, left)
        ext[a, first + 2, 16:24, 0:128] = roll(jnp.where(low, left, right), 4, 0)

    for a in range(count):
        for group in range(4):
            for r in range(2):
                slot = 2 * group + r
                place(a, 4 + 4 * group + r, ry[0, a, slot], ry[1, a, slot])
        for r in range(2):
            place(a, r, rxy[0, 0, a, r], rxy[0, 1, a, r])
            place(a, 20 + r, rxy[1, 0, a, r], rxy[1, 1, a, r])
        for part in range(3):
            for tile in range(3):
                both = []
                for zi in range(2):
                    if tile < 2:
                        both.append(rz[zi, a, tile] if part == 0 else rxz[part - 1, zi, a, tile])
                    elif part == 0:
                        both.append(jnp.where(low, ryz[1, zi, a], ryz[0, zi, a]))
                    else:
                        both.append(jnp.where(low, rxyz[part - 1, 1, zi, a], rxyz[part - 1, 0, zi, a]))
                comb = jnp.where(zleft, both[0], both[1])
                if part == 0:
                    pairs = [(4 + x, x) for x in range(16)]
                elif part == 1:
                    pairs = [(j, 12 + j) for j in range(4)]
                else:
                    pairs = [(20 + j, j) for j in range(4)]
                for plane, x in pairs:
                    ext[a, plane, 8 * tile : 8 * tile + 8, 128:256] = roll(comb, -(8 * x + 4), 1)


def planes_loop(first, last, unroll, body):
    total = last - first
    while total % unroll:
        unroll -= 1

    def step(i, carry):
        for u in range(unroll):
            body(first + i * unroll + u)
        return carry

    lax.fori_loop(0, total // unroll, step, 0)


def make_coefficients(load, coef, diag, inverse, x):
    k = load(x)
    faces = [0.5 * (k + load(x + 1)), 0.5 * (k + load(x - 1))]
    yp = 0.5 * (k + roll(k, -1, 0))
    zp = 0.5 * (k + roll(k, -1, 1))
    faces += [yp, roll(yp, 1, 0), zp, roll(zp, 1, 1)]
    d = SHIFT + ((faces[0] + faces[1]) + (faces[2] + faces[3]) + (faces[4] + faces[5]))
    inv = 1.0 / d
    for n in range(6):
        coef[n, x] = faces[n] * inv
    diag[x] = d
    inverse[x] = inv
    return inv


def scaled_residual(load, coef, scaled, x):
    v = load(x)
    total = scaled[x] - v
    total = total + (coef[0, x] * load(x + 1) + coef[1, x] * load(x - 1))
    total = total + (coef[2, x] * roll(v, -1, 0) + coef[3, x] * roll(v, 1, 0))
    total = total + (coef[4, x] * roll(v, -1, 1) + coef[5, x] * roll(v, 1, 1))
    return v, total


def shifts_plane(ref, ix):
    sub = iota((8, 8, 128), 1)
    lane = iota((8, 8, 128), 2)
    cur = ref[ix]
    nxt = jnp.concatenate([cur[1:], cur[:1]], axis=0)
    prv = jnp.concatenate([cur[7:], cur[:7]], axis=0)
    yp = jnp.where(sub % 4 == 3, roll(nxt, 3, 1), roll(cur, -1, 1))
    ym = jnp.where(sub % 4 == 0, roll(prv, -3, 1), roll(cur, 1, 1))
    half = roll(cur, 4, 1)
    swap = roll(half, 64, 2)
    swap_next = roll(roll(ref[(ix + 1) % 4], 4, 1), 64, 2)
    swap_prev = roll(roll(ref[(ix + 3) % 4], 4, 1), 64, 2)
    xp = jnp.where(sub < 4, half, jnp.where(lane < 64, swap, swap_next))
    xm = jnp.where(sub >= 4, half, jnp.where(lane >= 64, swap, swap_prev))
    return cur, (xp, xm, yp, ym, roll(cur, -1, 2), roll(cur, 1, 2))


def kernel(
    source, conductance, start, pressure, residual,
    ea, ev, va, vb, w0, fi0, coef0, diag0, inv0, py, pz, pyv, pzv,
    ry, rz, rxy, rxz, ryz, rxyz, ryv, rzv, rxyv, rxzv, ryzv, rxyzv,
    tk, tf, k1, v1a, v1b, w1, fi1, coef1, diag1, inv1,
    gk, gf, mk, mf, v2a, v2b, w2, coef2, diag2, inv2,
    ck, cf, k3, f3, v3a, v3b, w3, coef3,
    sem_s, sem_r, semv_s, semv_r, sem1,
):
    weights = chebyshev_weights(DEG, SMOOTH_FLOOR)
    coarse_weights = chebyshev_weights(COARSE_ITERS, COARSE_FLOOR)
    gx, gy, gz = (lax.axis_index(axis) for axis in AXES)
    recv = (ry, rz, rxy, rxz, ryz, rxyz)
    recv_v = (ryv, rzv, rxyv, rxzv, ryzv, rxyzv)

    everyone = list(dict.fromkeys(
        [tuple(s % n for s, n in zip(o, COUNT)) for o in NEAR + PLANE + RING]
    ))
    barrier = pltpu.get_barrier_semaphore()
    for offset in everyone:
        pl.semaphore_signal(barrier, inc=1, device_id=peer(offset), device_id_type=MESH)

    for a, ref in enumerate((start, conductance, source)):
        ea[a, 4:20, 0:16, 0:128] = ref[...]
    pack_fine(ea, 3, py, pz)
    pl.semaphore_wait(barrier, len(everyone))
    send_fine(ea, py, pz, recv, sem_s, sem_r)

    def restrict_fine(load, scale):
        rows = [
            jnp.concatenate([load(2 * p) + load(2 * p + 1), load(2 * p + 8) + load(2 * p + 9)], axis=1)
            for p in range(4)
        ]
        i, j = iota((256, 128), 0), iota((256, 128), 1)
        right = ones_where((i // 128 == j // 64) & ((i % 128) // 2 == j % 64), 0.125 * scale)
        mid = dot(jnp.concatenate(rows, axis=0), right)
        wide = jnp.concatenate([mid[16 * p : 16 * p + 16] for p in range(4)], axis=1)
        left = ones_where(iota((8, 16), 1) // 2 == iota((8, 16), 0))
        out = dot(left, wide)
        return [out[:, 128 * p : 128 * p + 128] for p in range(4)]

    def send_tile(tiles, pair):
        for offset in NEAR:
            slot = 9 * (1 - offset[0]) + 3 * (1 - offset[1]) + (1 - offset[2])
            send(tiles.at[13], tiles.at[slot], sem1.at[pair], sem1.at[pair + 1], offset)

    def unpack_tile(tiles, put):
        lane = iota((8, 128), 1)
        for i in range(3):
            for j in range(3):
                base = 9 * i + 3 * j
                for p in range(4):
                    own = tiles[base + 1, p]
                    side = jnp.where(lane % 64 < 32, tiles[base + 2, p], tiles[base, p])
                    put(8 * i + p, j, jnp.where(lane < 64, own, roll(side, 64, 1)))
                    put(8 * i + p + 4, j, jnp.where(lane < 64, roll(own, 64, 1), side))

    def restrict_middle(rows, scale):
        i, j = iota((16, 64), 0), iota((16, 64), 1)
        x = 2 * (i // 8) + (i % 8) // 4
        left = ones_where((j // 16 == x) & ((j % 8) // 2 == i % 4))
        mid = dot(left, rows)
        i, j = iota((256, 128), 0), iota((256, 128), 1)
        z = (16 + (i % 128) // 2) % 64
        right = ones_where((i // 128 == j // 64) & (z == j % 64), 0.125 * scale)
        return dot(jnp.concatenate([mid[0:8], mid[8:16]], axis=1), right)

    def send_plane(message, plane, pair):
        slot = gx * 8 + gy
        plane[slot] = message[...]
        for offset in PLANE:
            send(message, plane.at[slot], sem1.at[pair], sem1.at[pair + 1], offset)

    def restrict_plane(load, scale, message):
        i, j = iota((8, 32), 0), iota((8, 32), 1)
        left = ones_where((j // 8 == i // 2) & ((j % 4) // 2 == i % 2))
        i, j = iota((512, 128), 0), iota((512, 128), 1)
        z = i % 64
        right = ones_where(
            (i // 64 == j // 16) & (z >= 16) & (z < 48) & ((z - 16) // 2 == j % 16), 0.125 * scale
        )
        for tile in range(2):
            wide = jnp.concatenate(
                [load(ix)[4 * tile : 4 * tile + 4].reshape(32, 128) for ix in range(4)], axis=1
            )
            message[tile] = dot(dot(left, wide), right)

    def send_ring(message, ring, pair):
        ring[gz] = message[...]
        for offset in RING:
            send(message, ring.at[gz], sem1.at[pair], sem1.at[pair + 1], offset)

    def unpack_ring(ring, out):
        lane = iota((8, 128), 1)
        for x in range(8):
            for tile in range(2):
                acc = jnp.zeros((8, 128), F32)
                for z in range(8):
                    acc = jnp.where(lane // 16 == z, roll(ring[z, tile], 16 * (z - x), 1), acc)
                out[x, 8 * tile : 8 * tile + 8] = acc

    for p, block in enumerate(restrict_fine(lambda x: conductance[x], 0.25)):
        tk[13, p] = block
    send_tile(tk, 0)

    wait_fine(py, recv, sem_r)
    unpack_fine(ea, 3, recv)

    def fine_setup(x):
        inv = make_coefficients(lambda i: ea[1, i], coef0, diag0, inv0, x)
        fi0[x] = ea[2, x] * inv

    planes_loop(1, 23, 2, fine_setup)

    def fine_sweep(load, out, index, first, last, extra=None):
        carry, weight = weights[index]

        def body(x):
            v, r = scaled_residual(load, coef0, fi0, x)
            change = weight * r if index == 0 else carry * w0[x] + weight * r
            w0[x] = change
            out[x] = v + change
            if extra is not None:
                extra(x, v + change)

        planes_loop(first, last, 2, body)

    fine_sweep(lambda i: ea[0, i], va, 0, 1, 23)
    fine_sweep(lambda i: va[i], vb, 1, 2, 22)
    fine_sweep(lambda i: vb[i], va, 2, 3, 21)

    def fine_residual(x):
        v, r = scaled_residual(lambda i: va[i], coef0, fi0, x)
        vb[x] = r * diag0[x]
        ev[0, x, 0:16, 0:128] = v[0:16, 0:128]

    planes_loop(4, 20, 2, fine_residual)
    for p, block in enumerate(restrict_fine(lambda x: vb[4 + x, 0:16, 0:128], 1.0)):
        tf[13, p] = block
    send_tile(tf, 2)

    wait_bytes(tk.at[pl.ds(0, 26)], sem1.at[1])

    def put_k1(x, tile, value):
        k1[x, 8 * tile : 8 * tile + 8] = value

    unpack_tile(tk, put_k1)
    mk[...] = restrict_middle(k1[8:16, 8:16].reshape(64, 128), 0.25)
    send_plane(mk, gk, 4)
    pack_fine(ev, 1, pyv, pzv)
    send_fine(ev, pyv, pzv, recv_v, semv_s, semv_r)

    planes_loop(1, 23, 2, lambda x: make_coefficients(lambda i: k1[i], coef1, diag1, inv1, x))

    wait_bytes(tf.at[pl.ds(0, 26)], sem1.at[3])

    def put_f1(x, tile, value):
        fi1[x, 8 * tile : 8 * tile + 8] = value

    unpack_tile(tf, put_f1)

    def middle_first(x):
        scaled = fi1[x] * inv1[x]
        fi1[x] = scaled
        change = weights[0][1] * scaled
        w1[x] = change
        v1a[x] = change

    planes_loop(1, 23, 2, middle_first)

    def middle_sweep(load, out, index, first, last):
        carry, weight = weights[index]

        def body(x):
            v, r = scaled_residual(load, coef1, fi1, x)
            change = weight * r if index == 0 else carry * w1[x] + weight * r
            w1[x] = change
            out[x] = v + change

        planes_loop(first, last, 2, body)

    middle_sweep(lambda i: v1a[i], v1b, 1, 2, 22)
    middle_sweep(lambda i: v1b[i], v1a, 2, 3, 21)

    def middle_residual(x):
        _, r = scaled_residual(lambda i: v1a[i], coef1, fi1, x)
        v1b[x] = r * diag1[x]

    planes_loop(8, 16, 2, middle_residual)
    mf[...] = restrict_middle(v1b[8:16, 8:16].reshape(64, 128), 1.0)
    send_plane(mf, gf, 6)

    wait_bytes(gk.at[pl.ds(0, 31)], sem1.at[5])
    k2 = gk.reshape(4, 8, 8, 128)
    f2 = gf.reshape(4, 8, 8, 128)
    restrict_plane(lambda ix: k2[ix], 0.25, ck.at[8])
    send_ring(ck.at[8], ck, 8)
    for ix in range(4):
        k, around = shifts_plane(k2, ix)
        faces = [0.5 * (k + other) for other in around]
        d = SHIFT + ((faces[0] + faces[1]) + (faces[2] + faces[3]) + (faces[4] + faces[5]))
        inv = 1.0 / d
        for n in range(6):
            coef2[n, ix] = faces[n] * inv
        diag2[ix] = d
        inv2[ix] = inv

    wait_bytes(gf.at[pl.ds(0, 31)], sem1.at[7])
    for ix in range(4):
        change = weights[0][1] * (f2[ix] * inv2[ix])
        w2[ix] = change
        v2a[ix] = change

    def plane_residual(ref, ix):
        v, around = shifts_plane(ref, ix)
        total = f2[ix] * inv2[ix] - v
        for n in range(6):
            total = total + coef2[n, ix] * around[n]
        return v, total

    def plane_sweep(ref, out, index):
        carry, weight = weights[index]
        for ix in range(4):
            v, r = plane_residual(ref, ix)
            change = weight * r if index == 0 else carry * w2[ix] + weight * r
            w2[ix] = change
            out[ix] = v + change

    plane_sweep(v2a, v2b, 1)
    plane_sweep(v2b, v2a, 2)
    for ix in range(4):
        v2b[ix] = plane_residual(v2a, ix)[1] * diag2[ix]
    restrict_plane(lambda ix: v2b[ix], 1.0, cf.at[8])
    send_ring(cf.at[8], cf, 10)

    wait_bytes(ck.at[pl.ds(0, 7)], sem1.at[9])
    unpack_ring(ck, k3)
    for x in range(8):
        k = k3[x]
        faces = [0.5 * (k + k3[(x + 1) % 8]), 0.5 * (k + k3[(x + 7) % 8])]
        faces += [0.5 * (k + roll(k, s, dim)) for dim in (0, 1) for s in (-1, 1)]
        d = SHIFT + ((faces[0] + faces[1]) + (faces[2] + faces[3]) + (faces[4] + faces[5]))
        inv = 1.0 / d
        for n in range(6):
            coef3[n, x] = faces[n] * inv
        coef3[6, x] = inv
    wait_bytes(cf.at[pl.ds(0, 7)], sem1.at[11])
    unpack_ring(cf, f3)
    for x in range(8):
        scaled = f3[x] * coef3[6, x]
        f3[x] = scaled
        change = coarse_weights[0][1] * scaled
        w3[x] = change
        v3a[x] = change
    bufs = (v3a, v3b)
    for index in range(1, COARSE_ITERS):
        old, new = bufs[(index + 1) % 2], bufs[index % 2]
        carry, weight = coarse_weights[index]
        for x in range(8):
            v = old[x]
            total = f3[x] - v
            total = total + (coef3[0, x] * old[(x + 1) % 8] + coef3[1, x] * old[(x + 7) % 8])
            total = total + (coef3[2, x] * roll(v, -1, 0) + coef3[3, x] * roll(v, 1, 0))
            total = total + (coef3[4, x] * roll(v, -1, 1) + coef3[5, x] * roll(v, 1, 1))
            change = carry * w3[x] + weight * total
            w3[x] = change
            new[x] = v + change
    v3 = bufs[(COARSE_ITERS - 1) % 2]

    i, j = iota((256, 128), 0), iota((256, 128), 1)
    z = lax.rem(16 * gz + 120 + (j % 64) // 2, 128)
    right = ones_where((i // 128 == j // 64) & (i % 128 == z))
    rows = jnp.concatenate(
        [jnp.concatenate([v3[2 * ix], v3[2 * ix + 1]], axis=1) for ix in range(4)], axis=0
    )
    mid = dot(rows, right)
    wide = jnp.concatenate([mid[16 * ix : 16 * ix + 16] for ix in range(4)], axis=1)
    i, j = iota((64, 16), 0), iota((64, 16), 1)
    left = ones_where(j == 2 * (i // 8) + (i % 4) // 2)
    spread = dot(left, wide)
    for ix in range(4):
        v2b[ix] = v2a[ix] + spread[:, 128 * ix : 128 * ix + 128].reshape(8, 8, 128)
    plane_sweep(v2b, v2a, 0)
    plane_sweep(v2a, v2b, 1)
    plane_sweep(v2b, v2a, 2)

    tiles = [
        v2a[lax.rem(gx + i + 3, 4), lax.rem(gy + j + 7, 8)] for i in range(3) for j in range(3)
    ]
    i, j = iota((128, 256), 0), iota((128, 256), 1)
    right = ones_where((i // 64 == j // 128) & (i % 64 == (16 + (j % 128) // 2) % 64))
    mid = dot(jnp.concatenate(tiles, axis=0), right)
    wide = jnp.concatenate([mid[8 * t : 8 * t + 8] for t in range(9)], axis=1)
    i, j = iota((32, 8), 0), iota((32, 8), 1)
    left = ones_where(j == (i // 16) * 4 + (i % 8) // 2)
    spread = dot(left, wide)
    for t in range(9):
        for h in range(2):
            for x in range(4):
                plane = 8 * (t // 3) + 4 * h + x
                at = 8 * (t % 3)
                v1b[plane, at : at + 8] = (
                    v1a[plane, at : at + 8]
                    + spread[8 * x : 8 * x + 8, 256 * t + 128 * h : 256 * t + 128 * h + 128]
                )
    middle_sweep(lambda i: v1b[i], v1a, 0, 4, 20)
    middle_sweep(lambda i: v1a[i], v1b, 1, 5, 19)
    middle_sweep(lambda i: v1b[i], v1a, 2, 6, 18)

    wait_fine(pyv, recv_v, semv_r)
    unpack_fine(ev, 1, recv_v)
    wide = jnp.concatenate([v1a[6 + p] for p in range(12)], axis=1)
    i, j = iota((24, 24), 0), iota((24, 24), 1)
    left = ones_where(j == jnp.where(i < 20, 8 + i // 2, i // 2 - 4))
    mid = dot(left, wide)
    i, j = iota((128, 256), 0), iota((128, 256), 1)
    right = ones_where(i == j // 2)
    spread = dot(jnp.concatenate([mid[:, 128 * p : 128 * p + 128] for p in range(12)], axis=0), right)
    for p in range(12):
        for u in range(2):
            va[2 * p + u] = ev[0, 2 * p + u] + spread[24 * p : 24 * p + 24]
    fine_sweep(lambda i: va[i], vb, 0, 1, 23)
    fine_sweep(lambda i: vb[i], va, 1, 2, 22)
    fine_sweep(lambda i: va[i], vb, 2, 3, 21)

    def fine_last(x):
        v, r = scaled_residual(lambda i: vb[i], coef0, fi0, x)
        pressure[x - 4] = v[0:16, 0:128]
        residual[x - 4] = (r * diag0[x])[0:16, 0:128]

    planes_loop(4, 20, 2, fine_last)

    wait_fine(py, recv, sem_s)
    wait_fine(pyv, recv_v, semv_s)
    wait_bytes(tk.at[pl.ds(0, 26)], sem1.at[0])
    wait_bytes(tf.at[pl.ds(0, 26)], sem1.at[2])
    wait_bytes(gk.at[pl.ds(0, 31)], sem1.at[4])
    wait_bytes(gf.at[pl.ds(0, 31)], sem1.at[6])
    wait_bytes(ck.at[pl.ds(0, 7)], sem1.at[8])
    wait_bytes(cf.at[pl.ds(0, 7)], sem1.at[10])


def vmem(*shape):
    return pltpu.VMEM(shape, F32)


def fine_buffers(count):
    return [
        vmem(2, count, 8, 8, 128), vmem(2, count, 2, 8, 128), vmem(2, 2, count, 2, 8, 128),
        vmem(2, 2, count, 2, 8, 128), vmem(2, 2, count, 8, 128), vmem(2, 2, 2, count, 8, 128),
    ]


def per_device(source, conductance, pressure_start):
    fine = (24, 24, 256)
    middle = (24, 24, 128)
    plane = (4, 8, 8, 128)
    coarse = (8, 16, 128)
    scratch = [
        vmem(3, *fine), vmem(1, *fine), vmem(*fine), vmem(*fine), vmem(*fine), vmem(*fine),
        vmem(6, *fine), vmem(*fine), vmem(*fine),
        vmem(2, 3, 8, 8, 128), vmem(3, 2, 8, 128), vmem(2, 1, 8, 8, 128), vmem(1, 2, 8, 128),
    ]
    scratch += fine_buffers(3) + fine_buffers(1)
    scratch += [
        vmem(27, 4, 8, 128), vmem(27, 4, 8, 128), vmem(*middle), vmem(*middle), vmem(*middle),
        vmem(*middle), vmem(*middle), vmem(6, *middle), vmem(*middle), vmem(*middle),
        vmem(32, 8, 128), vmem(32, 8, 128), vmem(8, 128), vmem(8, 128),
        vmem(*plane), vmem(*plane), vmem(*plane), vmem(6, *plane), vmem(*plane), vmem(*plane),
        vmem(9, 2, 8, 128), vmem(9, 2, 8, 128), vmem(*coarse), vmem(*coarse), vmem(*coarse),
        vmem(*coarse), vmem(*coarse), vmem(7, *coarse),
        pltpu.SemaphoreType.DMA((7,)), pltpu.SemaphoreType.DMA((7,)),
        pltpu.SemaphoreType.DMA((7,)), pltpu.SemaphoreType.DMA((7,)),
        pltpu.SemaphoreType.DMA((12,)),
    ]
    block = jax.ShapeDtypeStruct(source.shape, F32)
    whole = pl.BlockSpec(memory_space=pltpu.VMEM)
    return pl.pallas_call(
        kernel,
        out_shape=(block, block),
        in_specs=[whole] * 3,
        out_specs=(whole, whole),
        scratch_shapes=scratch,
        compiler_params=pltpu.CompilerParams(
            collective_id=0, has_side_effects=True, vmem_limit_bytes=48 * 1024 * 1024
        ),
    )(source, conductance, pressure_start)


def solution(mesh):
    placed = (P("gx", "gy", "gz"), P("gx", "gy", "gz"), P("gx", "gy", "gz"))
    return jax.shard_map(
        per_device,
        mesh=mesh,
        in_specs=placed,
        out_specs=(P("gx", "gy", "gz"), P("gx", "gy", "gz")),
        check_vma=False,
    )
```

```python
import functools
import jax
import jax.numpy as jnp
from jax import lax
from jax.experimental import pallas as pl
from jax.experimental.pallas import tpu as pltpu
from jax.sharding import PartitionSpec as P

DEG = 3
COARSE_ITERS = 12
SHIFT = 0.001
UPPER_BOUND = 2.0
SMOOTH_FLOOR = 0.5
COARSE_FLOOR = 0.05

MESH = pl.DeviceIdType.MESH
AXES = ("gx", "gy", "gz")
COUNT = (4, 8, 8)
F32 = jnp.float32
SIGN = (1, -1)

NEAR = [
    (a, b, c)
    for c in (-1, 0, 1)
    for a in (-1, 0, 1)
    for b in (-1, 0, 1)
    if (a, b, c) != (0, 0, 0)
]
NEAR.sort(key=lambda o: -sum(map(abs, o)))
PLANE = [(a, b, 0) for a in range(4) for b in range(8) if (a, b) != (0, 0)]
RING = [(0, 0, c) for c in range(1, 8)]


def chebyshev_weights(number, floor_value):
    centre = 0.5 * (UPPER_BOUND + floor_value)
    half_width = 0.5 * (UPPER_BOUND - floor_value)
    ratio = centre / half_width
    factor = 1.0 / ratio
    weights = [(0.0, 1.0 / centre)]
    for _ in range(1, number):
        factor_next = 1.0 / (2.0 * ratio - factor)
        weights.append((factor_next * factor, 2.0 * factor_next / half_width))
        factor = factor_next
    return weights


def peer(offset):
    return tuple(
        lax.rem(lax.axis_index(axis) + (step + count), count)
        for axis, step, count in zip(AXES, offset, COUNT)
    )


def iota(shape, dim):
    return lax.broadcasted_iota(jnp.int32, shape, dim)


def roll(value, shift, dim):
    size = value.shape[dim]
    return pltpu.roll(value, shift % size, dim)


def dot(left, right):
    return jnp.dot(left, right, precision=lax.Precision.HIGHEST, preferred_element_type=F32)


def ones_where(mask, scale=1.0):
    return jnp.where(mask, F32(scale), F32(0.0))


def send(src, dst, ssem, rsem, offset):
    pltpu.make_async_remote_copy(
        src_ref=src, dst_ref=dst, send_sem=ssem, recv_sem=rsem,
        device_id=peer(offset), device_id_type=MESH,
    ).start()


def wait_bytes(ref, sem):
    pltpu.make_async_copy(ref, ref, sem).wait()


def pack_fine(ext, count, py, pz):
    sub = iota((8, 128), 0)
    lane = iota((8, 128), 1)
    for a in range(count):
        for group in range(4):
            for r in range(2):
                first = 4 + 4 * group + r
                slot = 2 * group + r
                py[0, a, slot] = jnp.where(
                    sub >= 4, ext[a, first, 8:16, 0:128], roll(ext[a, first + 2, 8:16, 0:128], 4, 0)
                )
                py[1, a, slot] = jnp.where(
                    sub < 4, ext[a, first, 0:8, 0:128], roll(ext[a, first + 2, 0:8, 0:128], 4, 0)
                )
        for tile in range(2):
            acc = jnp.zeros((8, 128), F32)
            for x in range(16):
                row = ext[a, 4 + x, 8 * tile : 8 * tile + 8, 0:128]
                acc = jnp.where(lane // 8 == x, roll(row, 8 * x + 4, 1), acc)
            pz[a, tile] = acc


def send_fine(ext, py, pz, recv, ssem, rsem):
    ry, rz, rxy, rxz, ryz, rxyz = recv
    for offset in NEAR:
        dx, dy, dz = offset
        xi, yi, zi = (0 if d == 1 else 1 for d in offset)
        kind = (dx != 0, dy != 0, dz != 0)
        tile = 1 if dy == 1 else 0
        planes = pl.ds(6, 2) if dx == 1 else pl.ds(0, 2)
        if kind == (True, False, False):
            src = ext.at[:, pl.ds(16 if dx == 1 else 4, 4), pl.ds(0, 16), pl.ds(0, 128)]
            dst = ext.at[:, pl.ds(0 if dx == 1 else 20, 4), pl.ds(0, 16), pl.ds(0, 128)]
            which = 0
        elif kind == (False, True, False):
            src, dst, which = py.at[yi], ry.at[yi], 1
        elif kind == (False, False, True):
            src, dst, which = pz, rz.at[zi], 2
        elif kind == (True, True, False):
            src, dst, which = py.at[yi, :, planes], rxy.at[xi, yi], 3
        elif kind == (True, False, True):
            src, dst, which = pz, rxz.at[xi, zi], 4
        elif kind == (False, True, True):
            src, dst, which = pz.at[:, tile], ryz.at[yi, zi], 5
        else:
            src, dst, which = pz.at[:, tile], rxyz.at[xi, yi, zi], 6
        send(src, dst, ssem.at[which], rsem.at[which], offset)


def wait_fine(py, recv, sem):
    refs = (recv[0].at[:, :, pl.ds(0, 8)],) + recv
    for which in range(7):
        wait_bytes(refs[which], sem.at[which])


def unpack_fine(ext, count, recv):
    ry, rz, rxy, rxz, ryz, rxyz = recv
    sub = iota((8, 128), 0)
    lane = iota((8, 128), 1)
    low = sub < 4
    zleft = lane % 8 < 4

    def place(a, first, left, right):
        ext[a, first, 16:24, 0:128] = jnp.where(low, right, left)
        ext[a, first + 2, 16:24, 0:128] = roll(jnp.where(low, left, right), 4, 0)

    for a in range(count):
        for group in range(4):
            for r in range(2):
                slot = 2 * group + r
                place(a, 4 + 4 * group + r, ry[0, a, slot], ry[1, a, slot])
        for r in range(2):
            place(a, r, rxy[0, 0, a, r], rxy[0, 1, a, r])
            place(a, 20 + r, rxy[1, 0, a, r], rxy[1, 1, a, r])
        for part in range(3):
            for tile in range(3):
                both = []
                for zi in range(2):
                    if tile < 2:
                        both.append(rz[zi, a, tile] if part == 0 else rxz[part - 1, zi, a, tile])
                    elif part == 0:
                        both.append(jnp.where(low, ryz[1, zi, a], ryz[0, zi, a]))
                    else:
                        both.append(jnp.where(low, rxyz[part - 1, 1, zi, a], rxyz[part - 1, 0, zi, a]))
                comb = jnp.where(zleft, both[0], both[1])
                if part == 0:
                    pairs = [(4 + x, x) for x in range(16)]
                elif part == 1:
                    pairs = [(j, 12 + j) for j in range(4)]
                else:
                    pairs = [(20 + j, j) for j in range(4)]
                for plane, x in pairs:
                    ext[a, plane, 8 * tile : 8 * tile + 8, 128:256] = roll(comb, -(8 * x + 4), 1)


def planes_loop(first, last, body):
    for x in range(first, last):
        body(x)


def make_coefficients(load, coef, diag, inverse, x):
    k = load(x)
    faces = [0.5 * (k + load(x + 1)), 0.5 * (k + load(x - 1))]
    yp = 0.5 * (k + roll(k, -1, 0))
    zp = 0.5 * (k + roll(k, -1, 1))
    faces += [yp, roll(yp, 1, 0), zp, roll(zp, 1, 1)]
    d = SHIFT + ((faces[0] + faces[1]) + (faces[2] + faces[3]) + (faces[4] + faces[5]))
    inv = 1.0 / d
    for n in range(6):
        coef[n, x] = faces[n] * inv
    diag[x] = d
    inverse[x] = inv
    return inv


def scaled_residual(load, coef, scaled, x):
    v = load(x)
    total = scaled[x] - v
    total = total + (coef[0, x] * load(x + 1) + coef[1, x] * load(x - 1))
    total = total + (coef[2, x] * roll(v, -1, 0) + coef[3, x] * roll(v, 1, 0))
    total = total + (coef[4, x] * roll(v, -1, 1) + coef[5, x] * roll(v, 1, 1))
    return v, total


def shifts_plane(ref, ix):
    sub = iota((8, 8, 128), 1)
    lane = iota((8, 8, 128), 2)
    cur = ref[ix]
    nxt = jnp.concatenate([cur[1:], cur[:1]], axis=0)
    prv = jnp.concatenate([cur[7:], cur[:7]], axis=0)
    yp = jnp.where(sub % 4 == 3, roll(nxt, 3, 1), roll(cur, -1, 1))
    ym = jnp.where(sub % 4 == 0, roll(prv, -3, 1), roll(cur, 1, 1))
    half = roll(cur, 4, 1)
    swap = roll(half, 64, 2)
    swap_next = roll(roll(ref[(ix + 1) % 4], 4, 1), 64, 2)
    swap_prev = roll(roll(ref[(ix + 3) % 4], 4, 1), 64, 2)
    xp = jnp.where(sub < 4, half, jnp.where(lane < 64, swap, swap_next))
    xm = jnp.where(sub >= 4, half, jnp.where(lane >= 64, swap, swap_prev))
    return cur, (xp, xm, yp, ym, roll(cur, -1, 2), roll(cur, 1, 2))


def kernel(
    source, conductance, start, pressure, residual,
    m_fine, m_middle, m_coarse, m_plane, m_tile, m_spread,
    ek, ea, ev, va, vb, w0, fi0, coef0, diag0, inv0, pyk, pzk, py, pz, pyv, pzv,
    ryk, rzk, rxyk, rxzk, ryzk, rxyzk,
    ry, rz, rxy, rxz, ryz, rxyz, ryv, rzv, rxyv, rxzv, ryzv, rxyzv,
    tk, tf, k1, v1a, v1b, w1, fi1, coef1, diag1, inv1,
    gk, gf, mk, mf, v2a, v2b, w2, coef2, diag2, inv2,
    ck, cf, k3, f3, v3a, v3b, w3, coef3,
    sem_in, semk_s, semk_r, sem_s, sem_r, semv_s, semv_r, sem1,
):
    weights = chebyshev_weights(DEG, SMOOTH_FLOOR)
    coarse_weights = chebyshev_weights(COARSE_ITERS, COARSE_FLOOR)
    gx, gy, gz = (lax.axis_index(axis) for axis in AXES)
    recv = (ry, rz, rxy, rxz, ryz, rxyz)
    recv_k = (ryk, rzk, rxyk, rxzk, ryzk, rxyzk)
    recv_v = (ryv, rzv, rxyv, rxzv, ryzv, rxyzv)

    everyone = list(dict.fromkeys(
        [tuple(s % n for s, n in zip(o, COUNT)) for o in NEAR + PLANE + RING]
    ))
    barrier = pltpu.get_barrier_semaphore()
    for offset in everyone:
        pl.semaphore_signal(barrier, inc=1, device_id=peer(offset), device_id_type=MESH)

    own = (pl.ds(4, 16), pl.ds(0, 16), pl.ds(0, 128))
    inputs = [
        pltpu.make_async_copy(ref, to.at[own], sem_in.at[n])
        for n, (ref, to) in enumerate(
            ((conductance, ek.at[0]), (start, ea.at[0]), (source, ea.at[1]))
        )
    ]
    for copy in inputs:
        copy.start()

    i, j = iota((256, 128), 0), iota((256, 128), 1)
    m_fine[...] = ones_where((i // 128 == j // 64) & ((i % 128) // 2 == j % 64), 0.125)
    m_middle[...] = ones_where(
        (i // 128 == j // 64) & ((16 + (i % 128) // 2) % 64 == j % 64), 0.125
    )
    z = lax.rem(16 * gz + 120 + (j % 64) // 2, 128)
    m_coarse[...] = ones_where((i // 128 == j // 64) & (i % 128 == z))
    i, j = iota((512, 128), 0), iota((512, 128), 1)
    z = i % 64
    m_plane[...] = ones_where(
        (i // 64 == j // 16) & (z >= 16) & (z < 48) & ((z - 16) // 2 == j % 16), 0.125
    )
    i, j = iota((128, 256), 0), iota((128, 256), 1)
    m_tile[...] = ones_where((i // 64 == j // 128) & (i % 64 == (16 + (j % 128) // 2) % 64))
    m_spread[...] = ones_where(i == j // 2)

    def restrict_fine(load, scale):
        rows = [
            jnp.concatenate([load(2 * p) + load(2 * p + 1), load(2 * p + 8) + load(2 * p + 9)], axis=1)
            for p in range(4)
        ]
        mid = dot(jnp.concatenate(rows, axis=0), m_fine[...])
        wide = jnp.concatenate([mid[16 * p : 16 * p + 16] for p in range(4)], axis=1)
        left = ones_where(iota((8, 16), 1) // 2 == iota((8, 16), 0))
        out = dot(left, wide)
        return [scale * out[:, 128 * p : 128 * p + 128] for p in range(4)]

    def send_tile(tiles, pair):
        for offset in NEAR:
            slot = 9 * (1 - offset[0]) + 3 * (1 - offset[1]) + (1 - offset[2])
            send(tiles.at[13], tiles.at[slot], sem1.at[pair], sem1.at[pair + 1], offset)

    def unpack_tile(tiles, put):
        lane = iota((8, 128), 1)
        for i in range(3):
            for j in range(3):
                base = 9 * i + 3 * j
                for p in range(4):
                    own = tiles[base + 1, p]
                    side = jnp.where(lane % 64 < 32, tiles[base + 2, p], tiles[base, p])
                    put(8 * i + p, j, jnp.where(lane < 64, own, roll(side, 64, 1)))
                    put(8 * i + p + 4, j, jnp.where(lane < 64, roll(own, 64, 1), side))

    def restrict_middle(rows, scale):
        i, j = iota((16, 64), 0), iota((16, 64), 1)
        x = 2 * (i // 8) + (i % 8) // 4
        left = ones_where((j // 16 == x) & ((j % 8) // 2 == i % 4))
        mid = dot(left, rows)
        return scale * dot(jnp.concatenate([mid[0:8], mid[8:16]], axis=1), m_middle[...])

    def send_plane(message, plane, pair):
        slot = gx * 8 + gy
        plane[slot] = message[...]
        for offset in PLANE:
            send(message, plane.at[slot], sem1.at[pair], sem1.at[pair + 1], offset)

    def restrict_plane(load, scale, message):
        i, j = iota((8, 32), 0), iota((8, 32), 1)
        left = ones_where((j // 8 == i // 2) & ((j % 4) // 2 == i % 2))
        for tile in range(2):
            wide = jnp.concatenate(
                [load(ix)[4 * tile : 4 * tile + 4].reshape(32, 128) for ix in range(4)], axis=1
            )
            message[tile] = scale * dot(dot(left, wide), m_plane[...])

    def send_ring(message, ring, pair):
        ring[gz] = message[...]
        for offset in RING:
            send(message, ring.at[gz], sem1.at[pair], sem1.at[pair + 1], offset)

    def unpack_ring(ring, out):
        lane = iota((8, 128), 1)
        for x in range(8):
            for tile in range(2):
                acc = jnp.zeros((8, 128), F32)
                for z in range(8):
                    acc = jnp.where(lane // 16 == z, roll(ring[z, tile], 16 * (z - x), 1), acc)
                out[x, 8 * tile : 8 * tile + 8] = acc

    inputs[0].wait()
    pack_fine(ek, 1, pyk, pzk)
    for p, block in enumerate(restrict_fine(lambda x: ek[0, 4 + x, 0:16, 0:128], 0.25)):
        tk[13, p] = block
    inputs[1].wait()
    inputs[2].wait()
    pack_fine(ea, 2, py, pz)
    pl.semaphore_wait(barrier, len(everyone))
    send_fine(ek, pyk, pzk, recv_k, semk_s, semk_r)
    send_fine(ea, py, pz, recv, sem_s, sem_r)

    wait_fine(pyk, recv_k, semk_r)
    unpack_fine(ek, 1, recv_k)
    planes_loop(1, 23, lambda x: make_coefficients(lambda i: ek[0, i], coef0, diag0, inv0, x))
    wait_fine(py, recv, sem_r)
    send_tile(tk, 0)
    unpack_fine(ea, 2, recv)

    def fine_scale(x):
        fi0[x] = ea[1, x] * inv0[x]

    planes_loop(1, 23, fine_scale)

    def fine_sweep(load, out, index, first, last, extra=None):
        carry, weight = weights[index]

        def body(x):
            v, r = scaled_residual(load, coef0, fi0, x)
            change = weight * r if index == 0 else carry * w0[x] + weight * r
            w0[x] = change
            out[x] = v + change
            if extra is not None:
                extra(x, v + change)

        planes_loop(first, last, body)

    fine_sweep(lambda i: ea[0, i], va, 0, 1, 23)
    fine_sweep(lambda i: va[i], vb, 1, 2, 22)
    fine_sweep(lambda i: vb[i], va, 2, 3, 21)

    def fine_residual(x):
        v, r = scaled_residual(lambda i: va[i], coef0, fi0, x)
        vb[x] = r * diag0[x]
        ev[0, x, 0:16, 0:128] = v[0:16, 0:128]

    planes_loop(4, 20, fine_residual)
    for p, block in enumerate(restrict_fine(lambda x: vb[4 + x, 0:16, 0:128], 1.0)):
        tf[13, p] = block
    send_tile(tf, 2)

    wait_bytes(tk.at[pl.ds(0, 26)], sem1.at[1])

    def put_k1(x, tile, value):
        k1[x, 8 * tile : 8 * tile + 8] = value

    unpack_tile(tk, put_k1)
    mk[...] = restrict_middle(k1[8:16, 8:16].reshape(64, 128), 0.25)
    send_plane(mk, gk, 4)
    planes_loop(1, 23, lambda x: make_coefficients(lambda i: k1[i], coef1, diag1, inv1, x))

    wait_bytes(tf.at[pl.ds(0, 26)], sem1.at[3])

    def put_f1(x, tile, value):
        fi1[x, 8 * tile : 8 * tile + 8] = value

    unpack_tile(tf, put_f1)

    def middle_first(x):
        scaled = fi1[x] * inv1[x]
        fi1[x] = scaled
        change = weights[0][1] * scaled
        w1[x] = change
        v1a[x] = change

    planes_loop(1, 23, middle_first)

    def middle_sweep(load, out, index, first, last):
        carry, weight = weights[index]

        def body(x):
            v, r = scaled_residual(load, coef1, fi1, x)
            change = weight * r if index == 0 else carry * w1[x] + weight * r
            w1[x] = change
            out[x] = v + change

        planes_loop(first, last, body)

    middle_sweep(lambda i: v1a[i], v1b, 1, 2, 22)
    middle_sweep(lambda i: v1b[i], v1a, 2, 3, 21)

    def middle_residual(x):
        _, r = scaled_residual(lambda i: v1a[i], coef1, fi1, x)
        v1b[x] = r * diag1[x]

    planes_loop(8, 16, middle_residual)
    mf[...] = restrict_middle(v1b[8:16, 8:16].reshape(64, 128), 1.0)
    send_plane(mf, gf, 6)
    pack_fine(ev, 1, pyv, pzv)
    send_fine(ev, pyv, pzv, recv_v, semv_s, semv_r)

    wait_bytes(gk.at[pl.ds(0, 31)], sem1.at[5])
    k2 = gk.reshape(4, 8, 8, 128)
    f2 = gf.reshape(4, 8, 8, 128)
    restrict_plane(lambda ix: k2[ix], 0.25, ck.at[8])
    send_ring(ck.at[8], ck, 8)
    for ix in range(4):
        k, around = shifts_plane(k2, ix)
        faces = [0.5 * (k + other) for other in around]
        d = SHIFT + ((faces[0] + faces[1]) + (faces[2] + faces[3]) + (faces[4] + faces[5]))
        inv = 1.0 / d
        for n in range(6):
            coef2[n, ix] = faces[n] * inv
        diag2[ix] = d
        inv2[ix] = inv

    wait_bytes(gf.at[pl.ds(0, 31)], sem1.at[7])
    for ix in range(4):
        change = weights[0][1] * (f2[ix] * inv2[ix])
        w2[ix] = change
        v2a[ix] = change

    def plane_residual(ref, ix):
        v, around = shifts_plane(ref, ix)
        total = f2[ix] * inv2[ix] - v
        for n in range(6):
            total = total + coef2[n, ix] * around[n]
        return v, total

    def plane_sweep(ref, out, index):
        carry, weight = weights[index]
        for ix in range(4):
            v, r = plane_residual(ref, ix)
            change = weight * r if index == 0 else carry * w2[ix] + weight * r
            w2[ix] = change
            out[ix] = v + change

    plane_sweep(v2a, v2b, 1)
    plane_sweep(v2b, v2a, 2)
    for ix in range(4):
        v2b[ix] = plane_residual(v2a, ix)[1] * diag2[ix]
    restrict_plane(lambda ix: v2b[ix], 1.0, cf.at[8])
    send_ring(cf.at[8], cf, 10)

    wait_bytes(ck.at[pl.ds(0, 7)], sem1.at[9])
    unpack_ring(ck, k3)
    for x in range(8):
        k = k3[x]
        faces = [0.5 * (k + k3[(x + 1) % 8]), 0.5 * (k + k3[(x + 7) % 8])]
        faces += [0.5 * (k + roll(k, s, dim)) for dim in (0, 1) for s in (-1, 1)]
        d = SHIFT + ((faces[0] + faces[1]) + (faces[2] + faces[3]) + (faces[4] + faces[5]))
        inv = 1.0 / d
        for n in range(6):
            coef3[n, x] = faces[n] * inv
        coef3[6, x] = inv
    wait_bytes(cf.at[pl.ds(0, 7)], sem1.at[11])
    unpack_ring(cf, f3)
    for x in range(8):
        scaled = f3[x] * coef3[6, x]
        f3[x] = scaled
        change = coarse_weights[0][1] * scaled
        w3[x] = change
        v3a[x] = change
    bufs = (v3a, v3b)
    for index in range(1, COARSE_ITERS):
        old, new = bufs[(index + 1) % 2], bufs[index % 2]
        carry, weight = coarse_weights[index]
        for x in range(8):
            v = old[x]
            total = f3[x] - v
            total = total + (coef3[0, x] * old[(x + 1) % 8] + coef3[1, x] * old[(x + 7) % 8])
            total = total + (coef3[2, x] * roll(v, -1, 0) + coef3[3, x] * roll(v, 1, 0))
            total = total + (coef3[4, x] * roll(v, -1, 1) + coef3[5, x] * roll(v, 1, 1))
            change = carry * w3[x] + weight * total
            w3[x] = change
            new[x] = v + change
    v3 = bufs[(COARSE_ITERS - 1) % 2]

    rows = jnp.concatenate(
        [jnp.concatenate([v3[2 * ix], v3[2 * ix + 1]], axis=1) for ix in range(4)], axis=0
    )
    mid = dot(rows, m_coarse[...])
    wide = jnp.concatenate([mid[16 * ix : 16 * ix + 16] for ix in range(4)], axis=1)
    i, j = iota((64, 16), 0), iota((64, 16), 1)
    left = ones_where(j == 2 * (i // 8) + (i % 4) // 2)
    spread = dot(left, wide)
    for ix in range(4):
        v2b[ix] = v2a[ix] + spread[:, 128 * ix : 128 * ix + 128].reshape(8, 8, 128)
    plane_sweep(v2b, v2a, 0)
    plane_sweep(v2a, v2b, 1)
    plane_sweep(v2b, v2a, 2)

    tiles = [
        v2a[lax.rem(gx + i + 3, 4), lax.rem(gy + j + 7, 8)] for i in range(3) for j in range(3)
    ]
    mid = dot(jnp.concatenate(tiles, axis=0), m_tile[...])
    wide = jnp.concatenate([mid[8 * t : 8 * t + 8] for t in range(9)], axis=1)
    i, j = iota((32, 8), 0), iota((32, 8), 1)
    left = ones_where(j == (i // 16) * 4 + (i % 8) // 2)
    spread = dot(left, wide)
    for t in range(9):
        for h in range(2):
            for x in range(4):
                plane = 8 * (t // 3) + 4 * h + x
                at = 8 * (t % 3)
                v1b[plane, at : at + 8] = (
                    v1a[plane, at : at + 8]
                    + spread[8 * x : 8 * x + 8, 256 * t + 128 * h : 256 * t + 128 * h + 128]
                )
    middle_sweep(lambda i: v1b[i], v1a, 0, 4, 20)
    middle_sweep(lambda i: v1a[i], v1b, 1, 5, 19)
    middle_sweep(lambda i: v1b[i], v1a, 2, 6, 18)

    wait_fine(pyv, recv_v, semv_r)
    unpack_fine(ev, 1, recv_v)
    wide = jnp.concatenate([v1a[6 + p] for p in range(12)], axis=1)
    i, j = iota((24, 24), 0), iota((24, 24), 1)
    left = ones_where(j == jnp.where(i < 20, 8 + i // 2, i // 2 - 4))
    mid = dot(left, wide)
    spread = dot(
        jnp.concatenate([mid[:, 128 * p : 128 * p + 128] for p in range(12)], axis=0), m_spread[...]
    )
    for p in range(12):
        for u in range(2):
            va[2 * p + u] = ev[0, 2 * p + u] + spread[24 * p : 24 * p + 24]
    fine_sweep(lambda i: va[i], vb, 0, 1, 23)
    fine_sweep(lambda i: vb[i], va, 1, 2, 22)
    fine_sweep(lambda i: va[i], vb, 2, 3, 21)

    def fine_last(x):
        v, r = scaled_residual(lambda i: vb[i], coef0, fi0, x)
        pressure[x - 4] = v[0:16, 0:128]
        residual[x - 4] = (r * diag0[x])[0:16, 0:128]

    planes_loop(4, 20, fine_last)

    wait_fine(pyk, recv_k, semk_s)
    wait_fine(py, recv, sem_s)
    wait_fine(pyv, recv_v, semv_s)
    wait_bytes(tk.at[pl.ds(0, 26)], sem1.at[0])
    wait_bytes(tf.at[pl.ds(0, 26)], sem1.at[2])
    wait_bytes(gk.at[pl.ds(0, 31)], sem1.at[4])
    wait_bytes(gf.at[pl.ds(0, 31)], sem1.at[6])
    wait_bytes(ck.at[pl.ds(0, 7)], sem1.at[8])
    wait_bytes(cf.at[pl.ds(0, 7)], sem1.at[10])


def vmem(*shape):
    return pltpu.VMEM(shape, F32)


def fine_buffers(count):
    return [
        vmem(2, count, 8, 8, 128), vmem(2, count, 2, 8, 128), vmem(2, 2, count, 2, 8, 128),
        vmem(2, 2, count, 2, 8, 128), vmem(2, 2, count, 8, 128), vmem(2, 2, 2, count, 8, 128),
    ]


def per_device(source, conductance, pressure_start):
    fine = (24, 24, 256)
    middle = (24, 24, 128)
    plane = (4, 8, 8, 128)
    coarse = (8, 16, 128)
    scratch = [
        vmem(256, 128), vmem(256, 128), vmem(256, 128), vmem(512, 128), vmem(128, 256), vmem(128, 256),
        vmem(1, *fine), vmem(2, *fine), vmem(1, *fine), vmem(*fine), vmem(*fine), vmem(*fine), vmem(*fine),
        vmem(6, *fine), vmem(*fine), vmem(*fine),
        vmem(2, 1, 8, 8, 128), vmem(1, 2, 8, 128), vmem(2, 2, 8, 8, 128), vmem(2, 2, 8, 128), vmem(2, 1, 8, 8, 128), vmem(1, 2, 8, 128),
    ]
    scratch += fine_buffers(1) + fine_buffers(2) + fine_buffers(1)
    scratch += [
        vmem(27, 4, 8, 128), vmem(27, 4, 8, 128), vmem(*middle), vmem(*middle), vmem(*middle),
        vmem(*middle), vmem(*middle), vmem(6, *middle), vmem(*middle), vmem(*middle),
        vmem(32, 8, 128), vmem(32, 8, 128), vmem(8, 128), vmem(8, 128),
        vmem(*plane), vmem(*plane), vmem(*plane), vmem(6, *plane), vmem(*plane), vmem(*plane),
        vmem(9, 2, 8, 128), vmem(9, 2, 8, 128), vmem(*coarse), vmem(*coarse), vmem(*coarse),
        vmem(*coarse), vmem(*coarse), vmem(7, *coarse),
        pltpu.SemaphoreType.DMA((3,)),
        pltpu.SemaphoreType.DMA((7,)), pltpu.SemaphoreType.DMA((7,)),
        pltpu.SemaphoreType.DMA((7,)), pltpu.SemaphoreType.DMA((7,)),
        pltpu.SemaphoreType.DMA((7,)), pltpu.SemaphoreType.DMA((7,)),
        pltpu.SemaphoreType.DMA((12,)),
    ]
    block = jax.ShapeDtypeStruct(source.shape, F32)
    whole = pl.BlockSpec(memory_space=pltpu.VMEM)
    return pl.pallas_call(
        kernel,
        out_shape=(block, block),
        in_specs=[pl.BlockSpec(memory_space=pltpu.HBM)] * 3,
        out_specs=(whole, whole),
        scratch_shapes=scratch,
        compiler_params=pltpu.CompilerParams(
            collective_id=0, has_side_effects=True, vmem_limit_bytes=48 * 1024 * 1024
        ),
    )(source, conductance, pressure_start)


def solution(mesh):
    placed = (P("gx", "gy", "gz"), P("gx", "gy", "gz"), P("gx", "gy", "gz"))
    return jax.shard_map(
        per_device,
        mesh=mesh,
        in_specs=placed,
        out_specs=(P("gx", "gy", "gz"), P("gx", "gy", "gz")),
        check_vma=False,
    )
```

```python
import functools
import jax
import jax.numpy as jnp
from jax import lax
from jax.experimental import pallas as pl
from jax.experimental.pallas import tpu as pltpu
from jax.sharding import PartitionSpec as P

DEG = 3
COARSE_ITERS = 12
SHIFT = 0.001
UPPER_BOUND = 2.0
SMOOTH_FLOOR = 0.5
COARSE_FLOOR = 0.05

MESH = pl.DeviceIdType.MESH
AXES = ("gx", "gy", "gz")
COUNT = (4, 8, 8)
F32 = jnp.float32
SIGN = (1, -1)

NEAR = [
    (a, b, c)
    for c in (-1, 0, 1)
    for a in (-1, 0, 1)
    for b in (-1, 0, 1)
    if (a, b, c) != (0, 0, 0)
]
NEAR.sort(key=lambda o: -sum(map(abs, o)))
PLANE = [(a, b, 0) for a in range(4) for b in range(8) if (a, b) != (0, 0)]
RING = [(0, 0, c) for c in range(1, 8)]


def chebyshev_weights(number, floor_value):
    centre = 0.5 * (UPPER_BOUND + floor_value)
    half_width = 0.5 * (UPPER_BOUND - floor_value)
    ratio = centre / half_width
    factor = 1.0 / ratio
    weights = [(0.0, 1.0 / centre)]
    for _ in range(1, number):
        factor_next = 1.0 / (2.0 * ratio - factor)
        weights.append((factor_next * factor, 2.0 * factor_next / half_width))
        factor = factor_next
    return weights


def peer(offset):
    return tuple(
        lax.rem(lax.axis_index(axis) + (step + count), count)
        for axis, step, count in zip(AXES, offset, COUNT)
    )


def iota(shape, dim):
    return lax.broadcasted_iota(jnp.int32, shape, dim)


def roll(value, shift, dim):
    size = value.shape[dim]
    return pltpu.roll(value, shift % size, dim)


def dot(left, right):
    return jnp.dot(left, right, precision=lax.Precision.HIGHEST, preferred_element_type=F32)


def ones_where(mask, scale=1.0):
    return jnp.where(mask, F32(scale), F32(0.0))


def send(src, dst, ssem, rsem, offset):
    pltpu.make_async_remote_copy(
        src_ref=src, dst_ref=dst, send_sem=ssem, recv_sem=rsem,
        device_id=peer(offset), device_id_type=MESH,
    ).start()


def wait_bytes(ref, sem):
    pltpu.make_async_copy(ref, ref, sem).wait()


def pack_fine(ext, count, py, pz, pw):
    sub = iota((8, 128), 0)
    lane = iota((8, 128), 1)
    for a in range(count):
        for group in range(4):
            for r in range(2):
                first = 4 + 4 * group + r
                slot = 2 * group + r
                py[0, a, slot] = jnp.where(
                    sub >= 4, ext[a, first, 8:16, 0:128], roll(ext[a, first + 2, 8:16, 0:128], 4, 0)
                )
                py[1, a, slot] = jnp.where(
                    sub < 4, ext[a, first, 0:8, 0:128], roll(ext[a, first + 2, 0:8, 0:128], 4, 0)
                )
        for tile in range(2):
            acc = jnp.zeros((8, 128), F32)
            for x in range(16):
                row = ext[a, 4 + x, 8 * tile : 8 * tile + 8, 0:128]
                acc = jnp.where(lane // 8 == x, roll(row, 8 * x + 4, 1), acc)
            pz[a, tile] = acc
    for side in range(2):
        acc = jnp.zeros((8, 128), F32)
        for a in range(count):
            for tile in range(2):
                at = 2 * a + tile
                acc = jnp.where(
                    lane // 32 == at, roll(pz[a, tile], 32 * at - (0 if side else 96), 1), acc
                )
        pw[side] = acc


def send_fine(ext, py, pz, pw, recv, ssem, rsem):
    ry, rz, rxy, rxz, ryz, rxyz = recv
    for offset in NEAR:
        dx, dy, dz = offset
        xi, yi, zi = (0 if d == 1 else 1 for d in offset)
        kind = (dx != 0, dy != 0, dz != 0)
        tile = 1 if dy == 1 else 0
        planes = pl.ds(6, 2) if dx == 1 else pl.ds(0, 2)
        if kind == (True, False, False):
            src = ext.at[:, pl.ds(16 if dx == 1 else 4, 4), pl.ds(0, 16), pl.ds(0, 128)]
            dst = ext.at[:, pl.ds(0 if dx == 1 else 20, 4), pl.ds(0, 16), pl.ds(0, 128)]
            which = 0
        elif kind == (False, True, False):
            src, dst, which = py.at[yi], ry.at[yi], 1
        elif kind == (False, False, True):
            src, dst, which = pz, rz.at[zi], 2
        elif kind == (True, True, False):
            src, dst, which = py.at[yi, :, planes], rxy.at[xi, yi], 3
        elif kind == (True, False, True):
            src, dst, which = pw.at[xi], rxz.at[xi, zi], 4
        elif kind == (False, True, True):
            src, dst, which = pz.at[:, tile], ryz.at[yi, zi], 5
        else:
            src, dst, which = pw.at[xi], rxyz.at[xi, yi, zi], 6
        send(src, dst, ssem.at[which], rsem.at[which], offset)


def wait_fine(py, recv, sem):
    refs = (recv[0].at[:, :, pl.ds(0, 8)],) + recv
    for which in range(7):
        wait_bytes(refs[which], sem.at[which])


def unpack_fine(ext, count, recv):
    ry, rz, rxy, rxz, ryz, rxyz = recv
    sub = iota((8, 128), 0)
    lane = iota((8, 128), 1)
    low = sub < 4
    zleft = lane % 8 < 4

    def place(a, first, left, right):
        ext[a, first, 16:24, 0:128] = jnp.where(low, right, left)
        ext[a, first + 2, 16:24, 0:128] = roll(jnp.where(low, left, right), 4, 0)

    for a in range(count):
        for group in range(4):
            for r in range(2):
                slot = 2 * group + r
                place(a, 4 + 4 * group + r, ry[0, a, slot], ry[1, a, slot])
        for r in range(2):
            place(a, r, rxy[0, 0, a, r], rxy[0, 1, a, r])
            place(a, 20 + r, rxy[1, 0, a, r], rxy[1, 1, a, r])
        for tile in range(3):
            both = []
            for zi in range(2):
                if tile < 2:
                    both.append(rz[zi, a, tile])
                else:
                    both.append(jnp.where(low, ryz[1, zi, a], ryz[0, zi, a]))
            comb = jnp.where(zleft, both[0], both[1])
            for x in range(16):
                ext[a, 4 + x, 8 * tile : 8 * tile + 8, 128:256] = roll(comb, -(8 * x + 4), 1)
    for side in range(2):
        edge = jnp.where(zleft, rxz[side, 0], rxz[side, 1])
        left = jnp.where(zleft, rxyz[side, 0, 0], rxyz[side, 0, 1])
        right = jnp.where(zleft, rxyz[side, 1, 0], rxyz[side, 1, 1])
        corner = jnp.where(low, right, roll(left, -32, 1))
        for a in range(count):
            for tile in range(3):
                for n in range(4):
                    value = roll(corner, -(64 * a + 8 * n + 4), 1) if tile == 2 else roll(
                        edge, -(32 * (2 * a + tile) + 8 * n + 4), 1
                    )
                    ext[a, 20 * side + n, 8 * tile : 8 * tile + 8, 128:256] = value


def planes_loop(first, last, body):
    for x in range(first, last):
        body(x)


def make_coefficients(load, coef, diag, inverse, x):
    k = load(x)
    faces = [0.5 * (k + load(x + 1)), 0.5 * (k + load(x - 1))]
    yp = 0.5 * (k + roll(k, -1, 0))
    zp = 0.5 * (k + roll(k, -1, 1))
    faces += [yp, roll(yp, 1, 0), zp, roll(zp, 1, 1)]
    d = SHIFT + ((faces[0] + faces[1]) + (faces[2] + faces[3]) + (faces[4] + faces[5]))
    inv = 1.0 / d
    for n in range(6):
        coef[n, x] = faces[n] * inv
    diag[x] = d
    inverse[x] = inv
    return inv


def scaled_residual(load, coef, scaled, x):
    v = load(x)
    total = scaled[x] - v
    total = total + (coef[0, x] * load(x + 1) + coef[1, x] * load(x - 1))
    total = total + (coef[2, x] * roll(v, -1, 0) + coef[3, x] * roll(v, 1, 0))
    total = total + (coef[4, x] * roll(v, -1, 1) + coef[5, x] * roll(v, 1, 1))
    return v, total


def shifts_plane(ref, ix):
    sub = iota((8, 8, 128), 1)
    lane = iota((8, 8, 128), 2)
    cur = ref[ix]
    nxt = jnp.concatenate([cur[1:], cur[:1]], axis=0)
    prv = jnp.concatenate([cur[7:], cur[:7]], axis=0)
    yp = jnp.where(sub % 4 == 3, roll(nxt, 3, 1), roll(cur, -1, 1))
    ym = jnp.where(sub % 4 == 0, roll(prv, -3, 1), roll(cur, 1, 1))
    half = roll(cur, 4, 1)
    swap = roll(half, 64, 2)
    swap_next = roll(roll(ref[(ix + 1) % 4], 4, 1), 64, 2)
    swap_prev = roll(roll(ref[(ix + 3) % 4], 4, 1), 64, 2)
    xp = jnp.where(sub < 4, half, jnp.where(lane < 64, swap, swap_next))
    xm = jnp.where(sub >= 4, half, jnp.where(lane >= 64, swap, swap_prev))
    return cur, (xp, xm, yp, ym, roll(cur, -1, 2), roll(cur, 1, 2))


def kernel(
    source, conductance, start, pressure, residual,
    m_fine, m_middle, m_coarse, m_plane, m_tile, m_spread,
    pwk, pw, pwv, ek, ea, ev, va, vb, w0, fi0, coef0, diag0, inv0, pyk, pzk, py, pz, pyv, pzv,
    ryk, rzk, rxyk, rxzk, ryzk, rxyzk,
    ry, rz, rxy, rxz, ryz, rxyz, ryv, rzv, rxyv, rxzv, ryzv, rxyzv,
    tk, tkz, zk, tf, tfz, zf, yf, yzf, nr, k1, v1a, v1b, w1, fi1, coef1, diag1, inv1,
    gk, gf, mk, mf, v2a, v2b, w2, coef2, diag2, inv2,
    ck, cf, k3, f3, v3a, v3b, w3, coef3,
    sem_in, semk_s, semk_r, sem_s, sem_r, semv_s, semv_r, sem1, semn,
):
    weights = chebyshev_weights(DEG, SMOOTH_FLOOR)
    coarse_weights = chebyshev_weights(COARSE_ITERS, COARSE_FLOOR)
    gx, gy, gz = (lax.axis_index(axis) for axis in AXES)
    recv = (ry, rz, rxy, rxz, ryz, rxyz)
    recv_k = (ryk, rzk, rxyk, rxzk, ryzk, rxyzk)
    recv_v = (ryv, rzv, rxyv, rxzv, ryzv, rxyzv)

    everyone = list(dict.fromkeys(
        [tuple(s % n for s, n in zip(o, COUNT)) for o in NEAR + RING + PLANE]
    ))
    barrier = pltpu.get_barrier_semaphore()
    for offset in everyone:
        pl.semaphore_signal(barrier, inc=1, device_id=peer(offset), device_id_type=MESH)

    own = (pl.ds(4, 16), pl.ds(0, 16), pl.ds(0, 128))
    inputs = [
        pltpu.make_async_copy(ref, to.at[own], sem_in.at[n])
        for n, (ref, to) in enumerate(
            ((conductance, ek.at[0]), (start, ea.at[0]), (source, ea.at[1]))
        )
    ]
    for copy in inputs:
        copy.start()

    def restrict_fine(load, scale):
        rows = [
            jnp.concatenate(
                [load(4 * p) + load(4 * p + 1), load(4 * p + 2) + load(4 * p + 3)], axis=1
            )
            for p in range(4)
        ]
        mid = dot(jnp.concatenate(rows, axis=0), m_fine[...])
        wide = jnp.concatenate([mid[16 * p : 16 * p + 16] for p in range(4)], axis=1)
        left = ones_where(iota((8, 16), 1) // 2 == iota((8, 16), 0))
        out = dot(left, wide)
        return [scale * out[:, 128 * p : 128 * p + 128] for p in range(4)]

    lane = iota((8, 128), 1)
    sub = iota((8, 128), 0)
    near_z = lane % 64 < 32
    near_y = sub < 4

    def half_z(first, second, which):
        if which == 0:
            return jnp.where(near_z, roll(second, -32, 1), first)
        return jnp.where(near_z, first, roll(second, 32, 1))

    def half_y(first, second, which):
        if which == 0:
            return jnp.where(near_y, roll(second, 4, 0), first)
        return jnp.where(near_y, first, roll(second, 4, 0))

    def sides(left, right):
        return (
            jnp.where(near_z, right, left),
            jnp.where(near_z, roll(right, -32, 1), roll(left, 32, 1)),
        )

    def place(put, x, tile, own, side):
        put(x, tile, jnp.where(lane < 64, own, roll(side, 64, 1)))
        put(x + 1, tile, jnp.where(lane < 64, roll(own, 64, 1), side))

    def pack_halves(tiles, zpack):
        for which in range(2):
            for n in range(2):
                zpack[which, n] = half_z(tiles[4, 2 * n], tiles[4, 2 * n + 1], which)

    def send_tile(tiles, zpack, ztiles, at):
        for dx, dy, dz in NEAR:
            slot = 3 * (1 - dx) + (1 - dy)
            if dz == 0:
                send(tiles.at[4], tiles.at[slot], sem1.at[at], sem1.at[at + 1], (dx, dy, dz))
            else:
                zi = 0 if dz == 1 else 1
                send(
                    zpack.at[zi], ztiles.at[zi, slot], sem1.at[at + 2], sem1.at[at + 3], (dx, dy, dz)
                )

    def wait_tile(tiles, ztiles, at):
        wait_bytes(tiles.at[pl.ds(0, 8)], sem1.at[at])
        wait_bytes(ztiles, sem1.at[at + 2])

    def unpack_tile(tiles, ztiles, put):
        for i in range(3):
            for j in range(3):
                base = 3 * i + j
                for n in range(2):
                    both = sides(ztiles[0, base, n], ztiles[1, base, n])
                    for r in range(2):
                        q = 2 * n + r
                        place(put, 8 * i + 2 * q, j, tiles[base, q], both[r])

    def near_slots(kind, xi, yi, zi):
        if kind == (True, False, False):
            return 2 * xi, 2
        if kind == (False, True, False):
            return 4 + 2 * yi, 2
        if kind == (False, False, True):
            return 8 + 2 * zi, 2
        if kind == (True, True, False):
            return 12 + 2 * xi + yi, 1
        if kind == (True, False, True):
            return 16 + 2 * xi + zi, 1
        if kind == (False, True, True):
            return 20 + 2 * yi + zi, 1
        return 24 + 4 * xi + 2 * yi + zi, 1

    def pack_near():
        pack_halves(tf, zf)
        for which in range(2):
            for n in range(2):
                yf[which, n] = half_y(tf[4, 2 * n], tf[4, 2 * n + 1], which)
            for other in range(2):
                yzf[which, other] = half_z(yf[which, 0], yf[which, 1], other)

    def send_near():
        for offset in NEAR:
            dx, dy, dz = offset
            xi, yi, zi = (0 if d == 1 else 1 for d in offset)
            kind = (dx != 0, dy != 0, dz != 0)
            at, size = near_slots(kind, xi, yi, zi)
            far = 1 - xi
            if kind == (True, False, False):
                src = tf.at[4, pl.ds(2 * far, 2)]
            elif kind == (False, True, False):
                src = yf.at[yi]
            elif kind == (False, False, True):
                src = zf.at[zi]
            elif kind == (True, True, False):
                src = yf.at[yi, pl.ds(far, 1)]
            elif kind == (True, False, True):
                src = zf.at[zi, pl.ds(far, 1)]
            else:
                src = yzf.at[yi, pl.ds(zi, 1)]
            send(src, nr.at[pl.ds(at, size)], semn.at[0], semn.at[1], offset)

    def unpack_near(put):
        def get(kind, xi, yi, zi, n=0):
            return nr[near_slots(kind, xi, yi, zi)[0] + n]

        x_, y_, z_ = (True, False, False), (False, True, False), (False, False, True)
        xy_, xz_, yz_, all_ = (True, True, False), (True, False, True), (False, True, True), (True,) * 3
        for n in range(2):
            both = sides(get(z_, 0, 0, 0, n), get(z_, 0, 0, 1, n))
            for r in range(2):
                place(put, 8 + 4 * n + 2 * r, 1, tf[4, 2 * n + r], both[r])
        for xi in range(2):
            first = 4 if xi == 0 else 16
            both = sides(get(xz_, xi, 0, 0), get(xz_, xi, 0, 1))
            for r in range(2):
                place(put, first + 2 * r, 1, get(x_, xi, 0, 0, r), both[r])
        for yi in range(2):
            tile = 2 * yi
            both = sides(get(yz_, 0, yi, 0), get(yz_, 0, yi, 1))
            for n in range(2):
                own = get(y_, 0, yi, 0, n)
                place(put, 8 + 4 * n, tile, own, both[n])
                place(put, 10 + 4 * n, tile, roll(own, 4, 0), roll(both[n], 4, 0))
            for xi in range(2):
                first = 4 if xi == 0 else 16
                side = sides(get(all_, xi, yi, 0), get(all_, xi, yi, 1))[1 - xi]
                own = get(xy_, xi, yi, 0)
                place(put, first, tile, own, side)
                place(put, first + 2, tile, roll(own, 4, 0), roll(side, 4, 0))

    def restrict_middle(rows, scale):
        i, j = iota((16, 64), 0), iota((16, 64), 1)
        x = 2 * (i // 8) + (i % 8) // 4
        left = ones_where((j // 16 == x) & ((j % 8) // 2 == i % 4))
        mid = dot(left, rows)
        return scale * dot(jnp.concatenate([mid[0:8], mid[8:16]], axis=1), m_middle[...])

    def send_plane(message, plane, pair):
        slot = gx * 8 + gy
        plane[slot] = message[...]
        for offset in PLANE:
            send(message, plane.at[slot], sem1.at[pair], sem1.at[pair + 1], offset)

    def restrict_plane(load, scale, message):
        i, j = iota((8, 32), 0), iota((8, 32), 1)
        left = ones_where((j // 8 == i // 2) & ((j % 4) // 2 == i % 2))
        for tile in range(2):
            wide = jnp.concatenate(
                [load(ix)[4 * tile : 4 * tile + 4].reshape(32, 128) for ix in range(4)], axis=1
            )
            message[tile] = scale * dot(dot(left, wide), m_plane[...])

    def send_ring(message, ring, pair):
        ring[gz] = message[...]
        for offset in RING:
            send(message, ring.at[gz], sem1.at[pair], sem1.at[pair + 1], offset)

    def unpack_ring(ring, out):
        lane = iota((8, 128), 1)
        for x in range(8):
            for tile in range(2):
                acc = jnp.zeros((8, 128), F32)
                for z in range(8):
                    acc = jnp.where(lane // 16 == z, roll(ring[z, tile], 16 * (z - x), 1), acc)
                out[x, 8 * tile : 8 * tile + 8] = acc

    inputs[0].wait()
    pack_fine(ek, 1, pyk, pzk, pwk)
    pl.semaphore_wait(barrier, len(everyone))
    send_fine(ek, pyk, pzk, pwk, recv_k, semk_s, semk_r)
    inputs[1].wait()
    inputs[2].wait()
    pack_fine(ea, 2, py, pz, pw)
    send_fine(ea, py, pz, pw, recv, sem_s, sem_r)

    i, j = iota((256, 128), 0), iota((256, 128), 1)
    m_fine[...] = ones_where((i // 128 == j // 64) & ((i % 128) // 2 == j % 64), 0.125)
    m_middle[...] = ones_where(
        (i // 128 == j // 64) & ((16 + (i % 128) // 2) % 64 == j % 64), 0.125
    )
    z = lax.rem(16 * gz + 120 + (j % 64) // 2, 128)
    m_coarse[...] = ones_where((i // 128 == j // 64) & (i % 128 == z))
    i, j = iota((512, 128), 0), iota((512, 128), 1)
    z = i % 64
    m_plane[...] = ones_where(
        (i // 64 == j // 16) & (z >= 16) & (z < 48) & ((z - 16) // 2 == j % 16), 0.125
    )
    i, j = iota((128, 256), 0), iota((128, 256), 1)
    m_tile[...] = ones_where((i // 64 == j // 128) & (i % 64 == (16 + (j % 128) // 2) % 64))
    m_spread[...] = ones_where(i == j // 2)
    for p, block in enumerate(restrict_fine(lambda x: ek[0, 4 + x, 0:16, 0:128], 0.25)):
        tk[4, p] = block
    pack_halves(tk, zk)
    wait_fine(pyk, recv_k, semk_r)
    unpack_fine(ek, 1, recv_k)
    planes_loop(1, 23, lambda x: make_coefficients(lambda i: ek[0, i], coef0, diag0, inv0, x))
    wait_fine(py, recv, sem_r)
    send_tile(tk, zk, tkz, 0)
    unpack_fine(ea, 2, recv)

    def fine_scale(x):
        fi0[x] = ea[1, x] * inv0[x]

    planes_loop(1, 23, fine_scale)

    def fine_sweep(load, out, index, first, last, extra=None):
        carry, weight = weights[index]

        def body(x):
            v, r = scaled_residual(load, coef0, fi0, x)
            change = weight * r if index == 0 else carry * w0[x] + weight * r
            w0[x] = change
            out[x] = v + change
            if extra is not None:
                extra(x, v + change)

        planes_loop(first, last, body)

    fine_sweep(lambda i: ea[0, i], va, 0, 1, 23)
    fine_sweep(lambda i: va[i], vb, 1, 2, 22)
    fine_sweep(lambda i: vb[i], va, 2, 3, 21)

    def fine_residual(x):
        v, r = scaled_residual(lambda i: va[i], coef0, fi0, x)
        vb[x] = r * diag0[x]
        ev[0, x, 0:16, 0:128] = v[0:16, 0:128]

    planes_loop(4, 20, fine_residual)
    for p, block in enumerate(restrict_fine(lambda x: vb[4 + x, 0:16, 0:128], 1.0)):
        tf[4, p] = block
    pack_near()
    send_near()

    wait_tile(tk, tkz, 1)

    def put_k1(x, tile, value):
        k1[x, 8 * tile : 8 * tile + 8] = value

    unpack_tile(tk, tkz, put_k1)
    mk[...] = restrict_middle(k1[8:16, 8:16].reshape(64, 128), 0.25)
    send_plane(mk, gk, 8)
    planes_loop(1, 23, lambda x: make_coefficients(lambda i: k1[i], coef1, diag1, inv1, x))

    wait_bytes(nr, semn.at[1])

    def put_f1(x, tile, value):
        fi1[x, 8 * tile : 8 * tile + 8] = value

    unpack_near(put_f1)

    def middle_first(x):
        scaled = fi1[x] * inv1[x]
        fi1[x] = scaled
        change = weights[0][1] * scaled
        w1[x] = change
        v1a[x] = change

    def middle_sweep(load, out, index, first, last):
        carry, weight = weights[index]

        def body(x):
            v, r = scaled_residual(load, coef1, fi1, x)
            change = weight * r if index == 0 else carry * w1[x] + weight * r
            w1[x] = change
            out[x] = v + change

        planes_loop(first, last, body)

    def middle_before(first, last):
        planes_loop(first, last, middle_first)
        middle_sweep(lambda i: v1a[i], v1b, 1, first + 1, last - 1)
        middle_sweep(lambda i: v1b[i], v1a, 2, first + 2, last - 2)

    middle_before(5, 19)

    def middle_residual(x):
        _, r = scaled_residual(lambda i: v1a[i], coef1, fi1, x)
        v1b[x] = r * diag1[x]

    planes_loop(8, 16, middle_residual)
    mf[...] = restrict_middle(v1b[8:16, 8:16].reshape(64, 128), 1.0)
    send_plane(mf, gf, 12)
    send_tile(tf, zf, tfz, 4)

    wait_bytes(gk.at[pl.ds(0, 31)], sem1.at[9])
    k2 = gk.reshape(4, 8, 8, 128)
    f2 = gf.reshape(4, 8, 8, 128)
    restrict_plane(lambda ix: k2[ix], 0.25, ck.at[8])
    send_ring(ck.at[8], ck, 10)
    for ix in range(4):
        k, around = shifts_plane(k2, ix)
        faces = [0.5 * (k + other) for other in around]
        d = SHIFT + ((faces[0] + faces[1]) + (faces[2] + faces[3]) + (faces[4] + faces[5]))
        inv = 1.0 / d
        for n in range(6):
            coef2[n, ix] = faces[n] * inv
        diag2[ix] = d
        inv2[ix] = inv

    wait_bytes(gf.at[pl.ds(0, 31)], sem1.at[13])
    for ix in range(4):
        change = weights[0][1] * (f2[ix] * inv2[ix])
        w2[ix] = change
        v2a[ix] = change

    def plane_residual(ref, ix):
        v, around = shifts_plane(ref, ix)
        total = f2[ix] * inv2[ix] - v
        for n in range(6):
            total = total + coef2[n, ix] * around[n]
        return v, total

    def plane_sweep(ref, out, index):
        carry, weight = weights[index]
        for ix in range(4):
            v, r = plane_residual(ref, ix)
            change = weight * r if index == 0 else carry * w2[ix] + weight * r
            w2[ix] = change
            out[ix] = v + change

    plane_sweep(v2a, v2b, 1)
    plane_sweep(v2b, v2a, 2)
    for ix in range(4):
        v2b[ix] = plane_residual(v2a, ix)[1] * diag2[ix]
    restrict_plane(lambda ix: v2b[ix], 1.0, cf.at[8])
    send_ring(cf.at[8], cf, 14)

    pack_fine(ev, 1, pyv, pzv, pwv)
    send_fine(ev, pyv, pzv, pwv, recv_v, semv_s, semv_r)
    wait_tile(tf, tfz, 5)
    unpack_tile(tf, tfz, put_f1)
    middle_before(1, 23)

    wait_bytes(ck.at[pl.ds(0, 7)], sem1.at[11])
    unpack_ring(ck, k3)
    for x in range(8):
        k = k3[x]
        faces = [0.5 * (k + k3[(x + 1) % 8]), 0.5 * (k + k3[(x + 7) % 8])]
        faces += [0.5 * (k + roll(k, s, dim)) for dim in (0, 1) for s in (-1, 1)]
        d = SHIFT + ((faces[0] + faces[1]) + (faces[2] + faces[3]) + (faces[4] + faces[5]))
        inv = 1.0 / d
        for n in range(6):
            coef3[n, x] = faces[n] * inv
        coef3[6, x] = inv
    wait_bytes(cf.at[pl.ds(0, 7)], sem1.at[15])
    unpack_ring(cf, f3)
    for x in range(8):
        scaled = f3[x] * coef3[6, x]
        f3[x] = scaled
        change = coarse_weights[0][1] * scaled
        w3[x] = change
        v3a[x] = change
    bufs = (v3a, v3b)
    for index in range(1, COARSE_ITERS):
        old, new = bufs[(index + 1) % 2], bufs[index % 2]
        carry, weight = coarse_weights[index]
        for x in range(8):
            v = old[x]
            total = f3[x] - v
            total = total + (coef3[0, x] * old[(x + 1) % 8] + coef3[1, x] * old[(x + 7) % 8])
            total = total + (coef3[2, x] * roll(v, -1, 0) + coef3[3, x] * roll(v, 1, 0))
            total = total + (coef3[4, x] * roll(v, -1, 1) + coef3[5, x] * roll(v, 1, 1))
            change = carry * w3[x] + weight * total
            w3[x] = change
            new[x] = v + change
    v3 = bufs[(COARSE_ITERS - 1) % 2]

    rows = jnp.concatenate(
        [jnp.concatenate([v3[2 * ix], v3[2 * ix + 1]], axis=1) for ix in range(4)], axis=0
    )
    mid = dot(rows, m_coarse[...])
    wide = jnp.concatenate([mid[16 * ix : 16 * ix + 16] for ix in range(4)], axis=1)
    i, j = iota((64, 16), 0), iota((64, 16), 1)
    left = ones_where(j == 2 * (i // 8) + (i % 4) // 2)
    spread = dot(left, wide)
    for ix in range(4):
        v2b[ix] = v2a[ix] + spread[:, 128 * ix : 128 * ix + 128].reshape(8, 8, 128)
    plane_sweep(v2b, v2a, 0)
    plane_sweep(v2a, v2b, 1)
    plane_sweep(v2b, v2a, 2)

    tiles = [
        v2a[lax.rem(gx + i + 3, 4), lax.rem(gy + j + 7, 8)] for i in range(3) for j in range(3)
    ]
    mid = dot(jnp.concatenate(tiles, axis=0), m_tile[...])
    wide = jnp.concatenate([mid[8 * t : 8 * t + 8] for t in range(9)], axis=1)
    i, j = iota((32, 8), 0), iota((32, 8), 1)
    left = ones_where(j == (i // 16) * 4 + (i % 8) // 2)
    spread = dot(left, wide)
    for t in range(9):
        for h in range(2):
            for x in range(4):
                plane = 8 * (t // 3) + 4 * h + x
                at = 8 * (t % 3)
                v1b[plane, at : at + 8] = (
                    v1a[plane, at : at + 8]
                    + spread[8 * x : 8 * x + 8, 256 * t + 128 * h : 256 * t + 128 * h + 128]
                )
    middle_sweep(lambda i: v1b[i], v1a, 0, 4, 20)
    middle_sweep(lambda i: v1a[i], v1b, 1, 5, 19)
    middle_sweep(lambda i: v1b[i], v1a, 2, 6, 18)

    wait_fine(pyv, recv_v, semv_r)
    unpack_fine(ev, 1, recv_v)
    wide = jnp.concatenate([v1a[6 + p] for p in range(12)], axis=1)
    i, j = iota((24, 24), 0), iota((24, 24), 1)
    left = ones_where(j == jnp.where(i < 20, 8 + i // 2, i // 2 - 4))
    mid = dot(left, wide)
    spread = dot(
        jnp.concatenate([mid[:, 128 * p : 128 * p + 128] for p in range(12)], axis=0), m_spread[...]
    )
    for p in range(12):
        for u in range(2):
            va[2 * p + u] = ev[0, 2 * p + u] + spread[24 * p : 24 * p + 24]
    fine_sweep(lambda i: va[i], vb, 0, 1, 23)
    fine_sweep(lambda i: vb[i], va, 1, 2, 22)
    fine_sweep(lambda i: va[i], vb, 2, 3, 21)

    def fine_last(x):
        v, r = scaled_residual(lambda i: vb[i], coef0, fi0, x)
        pressure[x - 4] = v[0:16, 0:128]
        residual[x - 4] = (r * diag0[x])[0:16, 0:128]

    planes_loop(4, 20, fine_last)

    wait_fine(pyk, recv_k, semk_s)
    wait_fine(py, recv, sem_s)
    wait_fine(pyv, recv_v, semv_s)
    wait_tile(tk, tkz, 0)
    wait_bytes(nr, semn.at[0])
    wait_tile(tf, tfz, 4)
    wait_bytes(gk.at[pl.ds(0, 31)], sem1.at[8])
    wait_bytes(ck.at[pl.ds(0, 7)], sem1.at[10])
    wait_bytes(gf.at[pl.ds(0, 31)], sem1.at[12])
    wait_bytes(cf.at[pl.ds(0, 7)], sem1.at[14])


def vmem(*shape):
    return pltpu.VMEM(shape, F32)


def fine_buffers(count):
    return [
        vmem(2, count, 8, 8, 128), vmem(2, count, 2, 8, 128), vmem(2, 2, count, 2, 8, 128),
        vmem(2, 2, 8, 128), vmem(2, 2, count, 8, 128), vmem(2, 2, 2, 8, 128),
    ]


def per_device(source, conductance, pressure_start):
    fine = (24, 24, 256)
    middle = (24, 24, 128)
    plane = (4, 8, 8, 128)
    coarse = (8, 16, 128)
    scratch = [
        vmem(256, 128), vmem(256, 128), vmem(256, 128), vmem(512, 128), vmem(128, 256), vmem(128, 256),
        vmem(2, 8, 128), vmem(2, 8, 128), vmem(2, 8, 128),
        vmem(1, *fine), vmem(2, *fine), vmem(1, *fine), vmem(*fine), vmem(*fine), vmem(*fine), vmem(*fine),
        vmem(6, *fine), vmem(*fine), vmem(*fine),
        vmem(2, 1, 8, 8, 128), vmem(1, 2, 8, 128), vmem(2, 2, 8, 8, 128), vmem(2, 2, 8, 128), vmem(2, 1, 8, 8, 128), vmem(1, 2, 8, 128),
    ]
    scratch += fine_buffers(1) + fine_buffers(2) + fine_buffers(1)
    scratch += [
        vmem(9, 4, 8, 128), vmem(2, 9, 2, 8, 128), vmem(2, 2, 8, 128),
        vmem(9, 4, 8, 128), vmem(2, 9, 2, 8, 128), vmem(2, 2, 8, 128),
        vmem(2, 2, 8, 128), vmem(2, 2, 8, 128), vmem(32, 8, 128), vmem(*middle), vmem(*middle), vmem(*middle),
        vmem(*middle), vmem(*middle), vmem(6, *middle), vmem(*middle), vmem(*middle),
        vmem(32, 8, 128), vmem(32, 8, 128), vmem(8, 128), vmem(8, 128),
        vmem(*plane), vmem(*plane), vmem(*plane), vmem(6, *plane), vmem(*plane), vmem(*plane),
        vmem(9, 2, 8, 128), vmem(9, 2, 8, 128), vmem(*coarse), vmem(*coarse), vmem(*coarse),
        vmem(*coarse), vmem(*coarse), vmem(7, *coarse),
        pltpu.SemaphoreType.DMA((3,)),
        pltpu.SemaphoreType.DMA((7,)), pltpu.SemaphoreType.DMA((7,)),
        pltpu.SemaphoreType.DMA((7,)), pltpu.SemaphoreType.DMA((7,)),
        pltpu.SemaphoreType.DMA((7,)), pltpu.SemaphoreType.DMA((7,)),
        pltpu.SemaphoreType.DMA((16,)), pltpu.SemaphoreType.DMA((2,)),
    ]
    block = jax.ShapeDtypeStruct(source.shape, F32)
    whole = pl.BlockSpec(memory_space=pltpu.VMEM)
    return pl.pallas_call(
        kernel,
        out_shape=(block, block),
        in_specs=[pl.BlockSpec(memory_space=pltpu.HBM)] * 3,
        out_specs=(whole, whole),
        scratch_shapes=scratch,
        compiler_params=pltpu.CompilerParams(
            collective_id=0, has_side_effects=True, vmem_limit_bytes=48 * 1024 * 1024
        ),
    )(source, conductance, pressure_start)


def solution(mesh):
    placed = (P("gx", "gy", "gz"), P("gx", "gy", "gz"), P("gx", "gy", "gz"))
    return jax.shard_map(
        per_device,
        mesh=mesh,
        in_specs=placed,
        out_specs=(P("gx", "gy", "gz"), P("gx", "gy", "gz")),
        check_vma=False,
    )
```

```python
import functools
import jax
import jax.numpy as jnp
from jax import lax
from jax.experimental import pallas as pl
from jax.experimental.pallas import tpu as pltpu
from jax.sharding import PartitionSpec as P

DEG = 3
COARSE_ITERS = 12
SHIFT = 0.001
UPPER_BOUND = 2.0
SMOOTH_FLOOR = 0.5
COARSE_FLOOR = 0.05

MESH = pl.DeviceIdType.MESH
AXES = ("gx", "gy", "gz")
COUNT = (4, 8, 8)
F32 = jnp.float32
SIGN = (1, -1)

NEAR = [
    (a, b, c)
    for c in (-1, 0, 1)
    for a in (-1, 0, 1)
    for b in (-1, 0, 1)
    if (a, b, c) != (0, 0, 0)
]
NEAR.sort(key=lambda o: -sum(map(abs, o)))
PLANE = [(a, b, 0) for a in range(4) for b in range(8) if (a, b) != (0, 0)]
RING = [(0, 0, c) for c in range(1, 8)]


def chebyshev_weights(number, floor_value):
    centre = 0.5 * (UPPER_BOUND + floor_value)
    half_width = 0.5 * (UPPER_BOUND - floor_value)
    ratio = centre / half_width
    factor = 1.0 / ratio
    weights = [(0.0, 1.0 / centre)]
    for _ in range(1, number):
        factor_next = 1.0 / (2.0 * ratio - factor)
        weights.append((factor_next * factor, 2.0 * factor_next / half_width))
        factor = factor_next
    return weights


def peer(offset):
    return tuple(
        lax.rem(lax.axis_index(axis) + (step + count), count)
        for axis, step, count in zip(AXES, offset, COUNT)
    )


def iota(shape, dim):
    return lax.broadcasted_iota(jnp.int32, shape, dim)


def roll(value, shift, dim):
    size = value.shape[dim]
    return pltpu.roll(value, shift % size, dim)


def parts_of(value):
    first = value.astype(jnp.bfloat16).astype(F32)
    rest = value - first
    second = rest.astype(jnp.bfloat16).astype(F32)
    return first, second, rest - second


def dot(value, matrix):
    rows = value.shape[0]
    out = jnp.dot(jnp.concatenate(parts_of(value), axis=0), matrix, preferred_element_type=F32)
    return (out[2 * rows :] + out[rows : 2 * rows]) + out[:rows]


def dot_rows(matrix, value):
    columns = value.shape[1]
    out = jnp.dot(matrix, jnp.concatenate(parts_of(value), axis=1), preferred_element_type=F32)
    return (out[:, 2 * columns :] + out[:, columns : 2 * columns]) + out[:, :columns]


def ones_where(mask, scale=1.0):
    return jnp.where(mask, F32(scale), F32(0.0))


def send(src, dst, ssem, rsem, offset):
    pltpu.make_async_remote_copy(
        src_ref=src, dst_ref=dst, send_sem=ssem, recv_sem=rsem,
        device_id=peer(offset), device_id_type=MESH,
    ).start()


def wait_bytes(ref, sem):
    pltpu.make_async_copy(ref, ref, sem).wait()


def pack_fine(ext, count, py, pz, pw):
    sub = iota((8, 128), 0)
    lane = iota((8, 128), 1)
    for a in range(count):
        for group in range(4):
            for r in range(2):
                first = 4 + 4 * group + r
                slot = 2 * group + r
                py[0, a, slot] = jnp.where(
                    sub >= 4, ext[a, first, 8:16, 0:128], roll(ext[a, first + 2, 8:16, 0:128], 4, 0)
                )
                py[1, a, slot] = jnp.where(
                    sub < 4, ext[a, first, 0:8, 0:128], roll(ext[a, first + 2, 0:8, 0:128], 4, 0)
                )
        for tile in range(2):
            acc = jnp.zeros((8, 128), F32)
            for x in range(16):
                row = ext[a, 4 + x, 8 * tile : 8 * tile + 8, 0:128]
                acc = jnp.where(lane // 8 == x, roll(row, 8 * x + 4, 1), acc)
            pz[a, tile] = acc
    for side in range(2):
        acc = jnp.zeros((8, 128), F32)
        for a in range(count):
            for tile in range(2):
                at = 2 * a + tile
                acc = jnp.where(
                    lane // 32 == at, roll(pz[a, tile], 32 * at - (0 if side else 96), 1), acc
                )
        pw[side] = acc


def send_fine(ext, py, pz, pw, recv, ssem, rsem):
    ry, rz, rxy, rxz, ryz, rxyz = recv
    for offset in NEAR:
        dx, dy, dz = offset
        xi, yi, zi = (0 if d == 1 else 1 for d in offset)
        kind = (dx != 0, dy != 0, dz != 0)
        tile = 1 if dy == 1 else 0
        planes = pl.ds(6, 2) if dx == 1 else pl.ds(0, 2)
        if kind == (True, False, False):
            src = ext.at[:, pl.ds(16 if dx == 1 else 4, 4), pl.ds(0, 16), pl.ds(0, 128)]
            dst = ext.at[:, pl.ds(0 if dx == 1 else 20, 4), pl.ds(0, 16), pl.ds(0, 128)]
            which = 0
        elif kind == (False, True, False):
            src, dst, which = py.at[yi], ry.at[yi], 1
        elif kind == (False, False, True):
            src, dst, which = pz, rz.at[zi], 2
        elif kind == (True, True, False):
            src, dst, which = py.at[yi, :, planes], rxy.at[xi, yi], 3
        elif kind == (True, False, True):
            src, dst, which = pw.at[xi], rxz.at[xi, zi], 4
        elif kind == (False, True, True):
            src, dst, which = pz.at[:, tile], ryz.at[yi, zi], 5
        else:
            src, dst, which = pw.at[xi], rxyz.at[xi, yi, zi], 6
        send(src, dst, ssem.at[which], rsem.at[which], offset)


def wait_fine(py, recv, sem):
    refs = (recv[0].at[:, :, pl.ds(0, 8)],) + recv
    for which in range(7):
        wait_bytes(refs[which], sem.at[which])


def unpack_fine(ext, count, recv):
    ry, rz, rxy, rxz, ryz, rxyz = recv
    sub = iota((8, 128), 0)
    lane = iota((8, 128), 1)
    low = sub < 4
    zleft = lane % 8 < 4

    def place(a, first, left, right):
        ext[a, first, 16:24, 0:128] = jnp.where(low, right, left)
        ext[a, first + 2, 16:24, 0:128] = roll(jnp.where(low, left, right), 4, 0)

    for a in range(count):
        for group in range(4):
            for r in range(2):
                slot = 2 * group + r
                place(a, 4 + 4 * group + r, ry[0, a, slot], ry[1, a, slot])
        for r in range(2):
            place(a, r, rxy[0, 0, a, r], rxy[0, 1, a, r])
            place(a, 20 + r, rxy[1, 0, a, r], rxy[1, 1, a, r])
        for tile in range(3):
            both = []
            for zi in range(2):
                if tile < 2:
                    both.append(rz[zi, a, tile])
                else:
                    both.append(jnp.where(low, ryz[1, zi, a], ryz[0, zi, a]))
            comb = jnp.where(zleft, both[0], both[1])
            for x in range(16):
                ext[a, 4 + x, 8 * tile : 8 * tile + 8, 128:256] = roll(comb, -(8 * x + 4), 1)
    for side in range(2):
        edge = jnp.where(zleft, rxz[side, 0], rxz[side, 1])
        left = jnp.where(zleft, rxyz[side, 0, 0], rxyz[side, 0, 1])
        right = jnp.where(zleft, rxyz[side, 1, 0], rxyz[side, 1, 1])
        corner = jnp.where(low, right, roll(left, -32, 1))
        for a in range(count):
            for tile in range(3):
                for n in range(4):
                    value = roll(corner, -(64 * a + 8 * n + 4), 1) if tile == 2 else roll(
                        edge, -(32 * (2 * a + tile) + 8 * n + 4), 1
                    )
                    ext[a, 20 * side + n, 8 * tile : 8 * tile + 8, 128:256] = value


def planes_loop(first, last, body):
    for x in range(first, last):
        body(x)


def make_coefficients(load, coef, diag, inverse, x):
    k = load(x)
    faces = [0.5 * (k + load(x + 1)), 0.5 * (k + load(x - 1))]
    yp = 0.5 * (k + roll(k, -1, 0))
    zp = 0.5 * (k + roll(k, -1, 1))
    faces += [yp, roll(yp, 1, 0), zp, roll(zp, 1, 1)]
    d = SHIFT + ((faces[0] + faces[1]) + (faces[2] + faces[3]) + (faces[4] + faces[5]))
    inv = 1.0 / d
    for n in range(6):
        coef[n, x] = faces[n] * inv
    diag[x] = d
    inverse[x] = inv
    return inv


def scaled_residual(load, coef, scaled, x):
    v = load(x)
    total = scaled[x] - v
    total = total + (coef[0, x] * load(x + 1) + coef[1, x] * load(x - 1))
    total = total + (coef[2, x] * roll(v, -1, 0) + coef[3, x] * roll(v, 1, 0))
    total = total + (coef[4, x] * roll(v, -1, 1) + coef[5, x] * roll(v, 1, 1))
    return v, total


def shifts_plane(ref, ix):
    sub = iota((8, 8, 128), 1)
    lane = iota((8, 8, 128), 2)
    cur = ref[ix]
    nxt = jnp.concatenate([cur[1:], cur[:1]], axis=0)
    prv = jnp.concatenate([cur[7:], cur[:7]], axis=0)
    yp = jnp.where(sub % 4 == 3, roll(nxt, 3, 1), roll(cur, -1, 1))
    ym = jnp.where(sub % 4 == 0, roll(prv, -3, 1), roll(cur, 1, 1))
    half = roll(cur, 4, 1)
    swap = roll(half, 64, 2)
    swap_next = roll(roll(ref[(ix + 1) % 4], 4, 1), 64, 2)
    swap_prev = roll(roll(ref[(ix + 3) % 4], 4, 1), 64, 2)
    xp = jnp.where(sub < 4, half, jnp.where(lane < 64, swap, swap_next))
    xm = jnp.where(sub >= 4, half, jnp.where(lane >= 64, swap, swap_prev))
    return cur, (xp, xm, yp, ym, roll(cur, -1, 2), roll(cur, 1, 2))


def kernel(
    source, conductance, start, pressure, residual,
    m_fine, m_middle, m_coarse, m_plane, m_tile, m_spread,
    pwk, pw, pwv, ek, ea, ev, va, vb, w0, fi0, coef0, diag0, inv0, pyk, pzk, py, pz, pyv, pzv,
    ryk, rzk, rxyk, rxzk, ryzk, rxyzk,
    ry, rz, rxy, rxz, ryz, rxyz, ryv, rzv, rxyv, rxzv, ryzv, rxyzv,
    tk, tkz, zk, tf, tfz, zf, yf, yzf, nr, k1, v1a, v1b, w1, fi1, coef1, diag1, inv1,
    gk, gf, mk, mf, v2a, v2b, w2, coef2, diag2, inv2,
    ck, cf, k3, f3, v3a, v3b, w3, coef3,
    sem_in, semk_s, semk_r, sem_s, sem_r, semv_s, semv_r, sem1, semn,
):
    weights = chebyshev_weights(DEG, SMOOTH_FLOOR)
    coarse_weights = chebyshev_weights(COARSE_ITERS, COARSE_FLOOR)
    gx, gy, gz = (lax.axis_index(axis) for axis in AXES)
    recv = (ry, rz, rxy, rxz, ryz, rxyz)
    recv_k = (ryk, rzk, rxyk, rxzk, ryzk, rxyzk)
    recv_v = (ryv, rzv, rxyv, rxzv, ryzv, rxyzv)

    everyone = list(dict.fromkeys(
        [tuple(s % n for s, n in zip(o, COUNT)) for o in NEAR + RING + PLANE]
    ))
    barrier = pltpu.get_barrier_semaphore()
    for offset in everyone:
        pl.semaphore_signal(barrier, inc=1, device_id=peer(offset), device_id_type=MESH)

    own = (pl.ds(4, 16), pl.ds(0, 16), pl.ds(0, 128))
    inputs = [
        pltpu.make_async_copy(ref, to.at[own], sem_in.at[n])
        for n, (ref, to) in enumerate(
            ((conductance, ek.at[0]), (start, ea.at[0]), (source, ea.at[1]))
        )
    ]
    for copy in inputs:
        copy.start()

    def restrict_fine(load, scale):
        rows = [
            jnp.concatenate(
                [load(4 * p) + load(4 * p + 1), load(4 * p + 2) + load(4 * p + 3)], axis=1
            )
            for p in range(4)
        ]
        mid = dot(jnp.concatenate(rows, axis=0), m_fine[...])
        wide = jnp.concatenate([mid[16 * p : 16 * p + 16] for p in range(4)], axis=1)
        left = ones_where(iota((8, 16), 1) // 2 == iota((8, 16), 0))
        out = dot_rows(left, wide)
        return [scale * out[:, 128 * p : 128 * p + 128] for p in range(4)]

    lane = iota((8, 128), 1)
    sub = iota((8, 128), 0)
    near_z = lane % 64 < 32
    near_y = sub < 4

    def half_z(first, second, which):
        if which == 0:
            return jnp.where(near_z, roll(second, -32, 1), first)
        return jnp.where(near_z, first, roll(second, 32, 1))

    def half_y(first, second, which):
        if which == 0:
            return jnp.where(near_y, roll(second, 4, 0), first)
        return jnp.where(near_y, first, roll(second, 4, 0))

    def sides(left, right):
        return (
            jnp.where(near_z, right, left),
            jnp.where(near_z, roll(right, -32, 1), roll(left, 32, 1)),
        )

    def place(put, x, tile, own, side):
        put(x, tile, jnp.where(lane < 64, own, roll(side, 64, 1)))
        put(x + 1, tile, jnp.where(lane < 64, roll(own, 64, 1), side))

    def pack_halves(tiles, zpack):
        for which in range(2):
            for n in range(2):
                zpack[which, n] = half_z(tiles[4, 2 * n], tiles[4, 2 * n + 1], which)

    def send_tile(tiles, zpack, ztiles, at):
        for dx, dy, dz in NEAR:
            slot = 3 * (1 - dx) + (1 - dy)
            if dz == 0:
                send(tiles.at[4], tiles.at[slot], sem1.at[at], sem1.at[at + 1], (dx, dy, dz))
            else:
                zi = 0 if dz == 1 else 1
                send(
                    zpack.at[zi], ztiles.at[zi, slot], sem1.at[at + 2], sem1.at[at + 3], (dx, dy, dz)
                )

    def wait_tile(tiles, ztiles, at):
        wait_bytes(tiles.at[pl.ds(0, 8)], sem1.at[at])
        wait_bytes(ztiles, sem1.at[at + 2])

    def unpack_tile(tiles, ztiles, put):
        for i in range(3):
            for j in range(3):
                base = 3 * i + j
                for n in range(2):
                    both = sides(ztiles[0, base, n], ztiles[1, base, n])
                    for r in range(2):
                        q = 2 * n + r
                        place(put, 8 * i + 2 * q, j, tiles[base, q], both[r])

    def near_slots(kind, xi, yi, zi):
        if kind == (True, False, False):
            return 2 * xi, 2
        if kind == (False, True, False):
            return 4 + 2 * yi, 2
        if kind == (False, False, True):
            return 8 + 2 * zi, 2
        if kind == (True, True, False):
            return 12 + 2 * xi + yi, 1
        if kind == (True, False, True):
            return 16 + 2 * xi + zi, 1
        if kind == (False, True, True):
            return 20 + 2 * yi + zi, 1
        return 24 + 4 * xi + 2 * yi + zi, 1

    def pack_near():
        pack_halves(tf, zf)
        for which in range(2):
            for n in range(2):
                yf[which, n] = half_y(tf[4, 2 * n], tf[4, 2 * n + 1], which)
            for other in range(2):
                yzf[which, other] = half_z(yf[which, 0], yf[which, 1], other)

    def send_near():
        for offset in NEAR:
            dx, dy, dz = offset
            xi, yi, zi = (0 if d == 1 else 1 for d in offset)
            kind = (dx != 0, dy != 0, dz != 0)
            at, size = near_slots(kind, xi, yi, zi)
            far = 1 - xi
            if kind == (True, False, False):
                src = tf.at[4, pl.ds(2 * far, 2)]
            elif kind == (False, True, False):
                src = yf.at[yi]
            elif kind == (False, False, True):
                src = zf.at[zi]
            elif kind == (True, True, False):
                src = yf.at[yi, pl.ds(far, 1)]
            elif kind == (True, False, True):
                src = zf.at[zi, pl.ds(far, 1)]
            else:
                src = yzf.at[yi, pl.ds(zi, 1)]
            send(src, nr.at[pl.ds(at, size)], semn.at[0], semn.at[1], offset)

    def unpack_near(put):
        def get(kind, xi, yi, zi, n=0):
            return nr[near_slots(kind, xi, yi, zi)[0] + n]

        x_, y_, z_ = (True, False, False), (False, True, False), (False, False, True)
        xy_, xz_, yz_, all_ = (True, True, False), (True, False, True), (False, True, True), (True,) * 3
        for n in range(2):
            both = sides(get(z_, 0, 0, 0, n), get(z_, 0, 0, 1, n))
            for r in range(2):
                place(put, 8 + 4 * n + 2 * r, 1, tf[4, 2 * n + r], both[r])
        for xi in range(2):
            first = 4 if xi == 0 else 16
            both = sides(get(xz_, xi, 0, 0), get(xz_, xi, 0, 1))
            for r in range(2):
                place(put, first + 2 * r, 1, get(x_, xi, 0, 0, r), both[r])
        for yi in range(2):
            tile = 2 * yi
            both = sides(get(yz_, 0, yi, 0), get(yz_, 0, yi, 1))
            for n in range(2):
                own = get(y_, 0, yi, 0, n)
                place(put, 8 + 4 * n, tile, own, both[n])
                place(put, 10 + 4 * n, tile, roll(own, 4, 0), roll(both[n], 4, 0))
            for xi in range(2):
                first = 4 if xi == 0 else 16
                side = sides(get(all_, xi, yi, 0), get(all_, xi, yi, 1))[1 - xi]
                own = get(xy_, xi, yi, 0)
                place(put, first, tile, own, side)
                place(put, first + 2, tile, roll(own, 4, 0), roll(side, 4, 0))

    def restrict_middle(rows, scale):
        i, j = iota((16, 64), 0), iota((16, 64), 1)
        x = 2 * (i // 8) + (i % 8) // 4
        left = ones_where((j // 16 == x) & ((j % 8) // 2 == i % 4))
        mid = dot_rows(left, rows)
        return scale * dot(jnp.concatenate([mid[0:8], mid[8:16]], axis=1), m_middle[...])

    def send_plane(message, plane, pair):
        slot = gx * 8 + gy
        plane[slot] = message[...]
        for offset in PLANE:
            send(message, plane.at[slot], sem1.at[pair], sem1.at[pair + 1], offset)

    def restrict_plane(load, scale, message):
        i, j = iota((8, 32), 0), iota((8, 32), 1)
        left = ones_where((j // 8 == i // 2) & ((j % 4) // 2 == i % 2))
        for tile in range(2):
            wide = jnp.concatenate(
                [load(ix)[4 * tile : 4 * tile + 4].reshape(32, 128) for ix in range(4)], axis=1
            )
            message[tile] = scale * dot(dot_rows(left, wide), m_plane[...])

    def send_ring(message, ring, pair):
        ring[gz] = message[...]
        for offset in RING:
            send(message, ring.at[gz], sem1.at[pair], sem1.at[pair + 1], offset)

    def unpack_ring(ring, out):
        lane = iota((8, 128), 1)
        for x in range(8):
            for tile in range(2):
                acc = jnp.zeros((8, 128), F32)
                for z in range(8):
                    acc = jnp.where(lane // 16 == z, roll(ring[z, tile], 16 * (z - x), 1), acc)
                out[x, 8 * tile : 8 * tile + 8] = acc

    inputs[0].wait()
    pack_fine(ek, 1, pyk, pzk, pwk)
    pl.semaphore_wait(barrier, len(everyone))
    send_fine(ek, pyk, pzk, pwk, recv_k, semk_s, semk_r)
    inputs[1].wait()
    inputs[2].wait()
    pack_fine(ea, 2, py, pz, pw)
    send_fine(ea, py, pz, pw, recv, sem_s, sem_r)

    i, j = iota((256, 128), 0), iota((256, 128), 1)
    m_fine[...] = ones_where((i // 128 == j // 64) & ((i % 128) // 2 == j % 64), 0.125)
    m_middle[...] = ones_where(
        (i // 128 == j // 64) & ((16 + (i % 128) // 2) % 64 == j % 64), 0.125
    )
    z = lax.rem(16 * gz + 120 + (j % 64) // 2, 128)
    m_coarse[...] = ones_where((i // 128 == j // 64) & (i % 128 == z))
    i, j = iota((512, 128), 0), iota((512, 128), 1)
    z = i % 64
    m_plane[...] = ones_where(
        (i // 64 == j // 16) & (z >= 16) & (z < 48) & ((z - 16) // 2 == j % 16), 0.125
    )
    i, j = iota((128, 256), 0), iota((128, 256), 1)
    m_tile[...] = ones_where((i // 64 == j // 128) & (i % 64 == (16 + (j % 128) // 2) % 64))
    m_spread[...] = ones_where(i == j // 2)
    for p, block in enumerate(restrict_fine(lambda x: ek[0, 4 + x, 0:16, 0:128], 0.25)):
        tk[4, p] = block
    pack_halves(tk, zk)
    wait_fine(pyk, recv_k, semk_r)
    unpack_fine(ek, 1, recv_k)
    planes_loop(1, 23, lambda x: make_coefficients(lambda i: ek[0, i], coef0, diag0, inv0, x))
    send_tile(tk, zk, tkz, 0)
    wait_fine(py, recv, sem_r)
    unpack_fine(ea, 2, recv)

    def fine_scale(x):
        fi0[x] = ea[1, x] * inv0[x]

    planes_loop(1, 23, fine_scale)

    def fine_sweep(load, out, index, first, last):
        carry, weight = weights[index]

        def body(x):
            v, r = scaled_residual(load, coef0, fi0, x)
            change = weight * r if index == 0 else carry * w0[x] + weight * r
            reach = 3 - index - max(4 - x, x - 19, 0)
            cuts = [(slice(0, 16), slice(0, 128))]
            if reach > 0:
                cuts += [(slice(16, 24), slice(0, 128)), (slice(0, 16), slice(128, 256))]
            if reach > 1:
                cuts += [(slice(16, 24), slice(128, 256))]
            for cut in cuts:
                if index < 2:
                    w0[(x,) + cut] = change[cut]
                out[(x,) + cut] = (v + change)[cut]

        planes_loop(first, last, body)

    fine_sweep(lambda i: ea[0, i], va, 0, 1, 23)
    fine_sweep(lambda i: va[i], vb, 1, 2, 22)
    fine_sweep(lambda i: vb[i], va, 2, 3, 21)

    def fine_residual(x):
        v, r = scaled_residual(lambda i: va[i], coef0, fi0, x)
        vb[x] = r * diag0[x]
        ev[0, x, 0:16, 0:128] = v[0:16, 0:128]

    planes_loop(4, 20, fine_residual)
    for p, block in enumerate(restrict_fine(lambda x: vb[4 + x, 0:16, 0:128], 1.0)):
        tf[4, p] = block
    pack_near()
    send_near()

    wait_tile(tk, tkz, 1)

    def put_k1(x, tile, value):
        k1[x, 8 * tile : 8 * tile + 8] = value

    unpack_tile(tk, tkz, put_k1)
    mk[...] = restrict_middle(k1[8:16, 8:16].reshape(64, 128), 0.25)
    send_plane(mk, gk, 8)
    planes_loop(1, 23, lambda x: make_coefficients(lambda i: k1[i], coef1, diag1, inv1, x))

    wait_bytes(nr, semn.at[1])

    def put_f1(x, tile, value):
        fi1[x, 8 * tile : 8 * tile + 8] = value

    unpack_near(put_f1)

    def middle_first(x):
        scaled = fi1[x] * inv1[x]
        fi1[x] = scaled
        change = weights[0][1] * scaled
        w1[x] = change
        v1a[x] = change

    def middle_sweep(load, out, index, first, last):
        carry, weight = weights[index]

        def body(x):
            v, r = scaled_residual(load, coef1, fi1, x)
            change = weight * r if index == 0 else carry * w1[x] + weight * r
            w1[x] = change
            out[x] = v + change

        planes_loop(first, last, body)

    def middle_before(first, last):
        planes_loop(first, last, middle_first)
        middle_sweep(lambda i: v1a[i], v1b, 1, first + 1, last - 1)
        middle_sweep(lambda i: v1b[i], v1a, 2, first + 2, last - 2)

    middle_before(5, 19)

    def middle_residual(x):
        _, r = scaled_residual(lambda i: v1a[i], coef1, fi1, x)
        v1b[x] = r * diag1[x]

    planes_loop(8, 16, middle_residual)
    mf[...] = restrict_middle(v1b[8:16, 8:16].reshape(64, 128), 1.0)
    send_plane(mf, gf, 12)
    send_tile(tf, zf, tfz, 4)

    wait_bytes(gk.at[pl.ds(0, 31)], sem1.at[9])
    k2 = gk.reshape(4, 8, 8, 128)
    f2 = gf.reshape(4, 8, 8, 128)
    restrict_plane(lambda ix: k2[ix], 0.25, ck.at[8])
    send_ring(ck.at[8], ck, 10)
    for ix in range(4):
        k, around = shifts_plane(k2, ix)
        faces = [0.5 * (k + other) for other in around]
        d = SHIFT + ((faces[0] + faces[1]) + (faces[2] + faces[3]) + (faces[4] + faces[5]))
        inv = 1.0 / d
        for n in range(6):
            coef2[n, ix] = faces[n] * inv
        diag2[ix] = d
        inv2[ix] = inv

    wait_bytes(gf.at[pl.ds(0, 31)], sem1.at[13])
    for ix in range(4):
        change = weights[0][1] * (f2[ix] * inv2[ix])
        w2[ix] = change
        v2a[ix] = change

    def plane_residual(ref, ix):
        v, around = shifts_plane(ref, ix)
        total = f2[ix] * inv2[ix] - v
        for n in range(6):
            total = total + coef2[n, ix] * around[n]
        return v, total

    def plane_sweep(ref, out, index):
        carry, weight = weights[index]
        for ix in range(4):
            v, r = plane_residual(ref, ix)
            change = weight * r if index == 0 else carry * w2[ix] + weight * r
            w2[ix] = change
            out[ix] = v + change

    plane_sweep(v2a, v2b, 1)
    plane_sweep(v2b, v2a, 2)
    for ix in range(4):
        v2b[ix] = plane_residual(v2a, ix)[1] * diag2[ix]
    restrict_plane(lambda ix: v2b[ix], 1.0, cf.at[8])
    send_ring(cf.at[8], cf, 14)

    pack_fine(ev, 1, pyv, pzv, pwv)
    send_fine(ev, pyv, pzv, pwv, recv_v, semv_s, semv_r)
    wait_tile(tf, tfz, 5)
    unpack_tile(tf, tfz, put_f1)
    middle_before(1, 23)

    wait_bytes(ck.at[pl.ds(0, 7)], sem1.at[11])
    unpack_ring(ck, k3)
    for x in range(8):
        k = k3[x]
        faces = [0.5 * (k + k3[(x + 1) % 8]), 0.5 * (k + k3[(x + 7) % 8])]
        faces += [0.5 * (k + roll(k, s, dim)) for dim in (0, 1) for s in (-1, 1)]
        d = SHIFT + ((faces[0] + faces[1]) + (faces[2] + faces[3]) + (faces[4] + faces[5]))
        inv = 1.0 / d
        for n in range(6):
            coef3[n, x] = faces[n] * inv
        coef3[6, x] = inv
    wait_bytes(cf.at[pl.ds(0, 7)], sem1.at[15])
    unpack_ring(cf, f3)
    for x in range(8):
        scaled = f3[x] * coef3[6, x]
        f3[x] = scaled
        change = coarse_weights[0][1] * scaled
        w3[x] = change
        v3a[x] = change
    bufs = (v3a, v3b)
    for index in range(1, COARSE_ITERS):
        old, new = bufs[(index + 1) % 2], bufs[index % 2]
        carry, weight = coarse_weights[index]
        for x in range(8):
            v = old[x]
            total = f3[x] - v
            total = total + (coef3[0, x] * old[(x + 1) % 8] + coef3[1, x] * old[(x + 7) % 8])
            total = total + (coef3[2, x] * roll(v, -1, 0) + coef3[3, x] * roll(v, 1, 0))
            total = total + (coef3[4, x] * roll(v, -1, 1) + coef3[5, x] * roll(v, 1, 1))
            change = carry * w3[x] + weight * total
            w3[x] = change
            new[x] = v + change
    v3 = bufs[(COARSE_ITERS - 1) % 2]

    rows = jnp.concatenate(
        [jnp.concatenate([v3[2 * ix], v3[2 * ix + 1]], axis=1) for ix in range(4)], axis=0
    )
    mid = dot(rows, m_coarse[...])
    wide = jnp.concatenate([mid[16 * ix : 16 * ix + 16] for ix in range(4)], axis=1)
    i, j = iota((64, 16), 0), iota((64, 16), 1)
    left = ones_where(j == 2 * (i // 8) + (i % 4) // 2)
    spread = dot_rows(left, wide)
    for ix in range(4):
        v2b[ix] = v2a[ix] + spread[:, 128 * ix : 128 * ix + 128].reshape(8, 8, 128)
    plane_sweep(v2b, v2a, 0)
    plane_sweep(v2a, v2b, 1)
    plane_sweep(v2b, v2a, 2)

    tiles = [
        v2a[lax.rem(gx + i + 3, 4), lax.rem(gy + j + 7, 8)] for i in range(3) for j in range(3)
    ]
    mid = dot(jnp.concatenate(tiles, axis=0), m_tile[...])
    wide = jnp.concatenate([mid[8 * t : 8 * t + 8] for t in range(9)], axis=1)
    i, j = iota((32, 8), 0), iota((32, 8), 1)
    left = ones_where(j == (i // 16) * 4 + (i % 8) // 2)
    spread = dot_rows(left, wide)
    for t in range(9):
        for h in range(2):
            for x in range(4):
                plane = 8 * (t // 3) + 4 * h + x
                at = 8 * (t % 3)
                v1b[plane, at : at + 8] = (
                    v1a[plane, at : at + 8]
                    + spread[8 * x : 8 * x + 8, 256 * t + 128 * h : 256 * t + 128 * h + 128]
                )
    middle_sweep(lambda i: v1b[i], v1a, 0, 4, 20)
    middle_sweep(lambda i: v1a[i], v1b, 1, 5, 19)
    middle_sweep(lambda i: v1b[i], v1a, 2, 6, 18)

    wait_fine(pyv, recv_v, semv_r)
    unpack_fine(ev, 1, recv_v)
    wide = jnp.concatenate([v1a[6 + p] for p in range(12)], axis=1)
    i, j = iota((24, 24), 0), iota((24, 24), 1)
    left = ones_where(j == jnp.where(i < 20, 8 + i // 2, i // 2 - 4))
    mid = dot_rows(left, wide)
    spread = dot(
        jnp.concatenate([mid[:, 128 * p : 128 * p + 128] for p in range(12)], axis=0), m_spread[...]
    )
    for p in range(12):
        for u in range(2):
            va[2 * p + u] = ev[0, 2 * p + u] + spread[24 * p : 24 * p + 24]
    fine_sweep(lambda i: va[i], vb, 0, 1, 23)
    fine_sweep(lambda i: vb[i], va, 1, 2, 22)
    fine_sweep(lambda i: va[i], vb, 2, 3, 21)

    def fine_last(x):
        v, r = scaled_residual(lambda i: vb[i], coef0, fi0, x)
        pressure[x - 4] = v[0:16, 0:128]
        residual[x - 4] = (r * diag0[x])[0:16, 0:128]

    planes_loop(4, 20, fine_last)

    wait_fine(pyk, recv_k, semk_s)
    wait_fine(py, recv, sem_s)
    wait_fine(pyv, recv_v, semv_s)
    wait_tile(tk, tkz, 0)
    wait_bytes(nr, semn.at[0])
    wait_tile(tf, tfz, 4)
    wait_bytes(gk.at[pl.ds(0, 31)], sem1.at[8])
    wait_bytes(ck.at[pl.ds(0, 7)], sem1.at[10])
    wait_bytes(gf.at[pl.ds(0, 31)], sem1.at[12])
    wait_bytes(cf.at[pl.ds(0, 7)], sem1.at[14])


def vmem(*shape):
    return pltpu.VMEM(shape, F32)


def fine_buffers(count):
    return [
        vmem(2, count, 8, 8, 128), vmem(2, count, 2, 8, 128), vmem(2, 2, count, 2, 8, 128),
        vmem(2, 2, 8, 128), vmem(2, 2, count, 8, 128), vmem(2, 2, 2, 8, 128),
    ]


def per_device(source, conductance, pressure_start):
    fine = (24, 24, 256)
    middle = (24, 24, 128)
    plane = (4, 8, 8, 128)
    coarse = (8, 16, 128)
    scratch = [
        vmem(256, 128), vmem(256, 128), vmem(256, 128), vmem(512, 128), vmem(128, 256), vmem(128, 256),
        vmem(2, 8, 128), vmem(2, 8, 128), vmem(2, 8, 128),
        vmem(1, *fine), vmem(2, *fine), vmem(1, *fine), vmem(*fine), vmem(*fine), vmem(*fine), vmem(*fine),
        vmem(6, *fine), vmem(*fine), vmem(*fine),
        vmem(2, 1, 8, 8, 128), vmem(1, 2, 8, 128), vmem(2, 2, 8, 8, 128), vmem(2, 2, 8, 128), vmem(2, 1, 8, 8, 128), vmem(1, 2, 8, 128),
    ]
    scratch += fine_buffers(1) + fine_buffers(2) + fine_buffers(1)
    scratch += [
        vmem(9, 4, 8, 128), vmem(2, 9, 2, 8, 128), vmem(2, 2, 8, 128),
        vmem(9, 4, 8, 128), vmem(2, 9, 2, 8, 128), vmem(2, 2, 8, 128),
        vmem(2, 2, 8, 128), vmem(2, 2, 8, 128), vmem(32, 8, 128), vmem(*middle), vmem(*middle), vmem(*middle),
        vmem(*middle), vmem(*middle), vmem(6, *middle), vmem(*middle), vmem(*middle),
        vmem(32, 8, 128), vmem(32, 8, 128), vmem(8, 128), vmem(8, 128),
        vmem(*plane), vmem(*plane), vmem(*plane), vmem(6, *plane), vmem(*plane), vmem(*plane),
        vmem(9, 2, 8, 128), vmem(9, 2, 8, 128), vmem(*coarse), vmem(*coarse), vmem(*coarse),
        vmem(*coarse), vmem(*coarse), vmem(7, *coarse),
        pltpu.SemaphoreType.DMA((3,)),
        pltpu.SemaphoreType.DMA((7,)), pltpu.SemaphoreType.DMA((7,)),
        pltpu.SemaphoreType.DMA((7,)), pltpu.SemaphoreType.DMA((7,)),
        pltpu.SemaphoreType.DMA((7,)), pltpu.SemaphoreType.DMA((7,)),
        pltpu.SemaphoreType.DMA((16,)), pltpu.SemaphoreType.DMA((2,)),
    ]
    block = jax.ShapeDtypeStruct(source.shape, F32)
    whole = pl.BlockSpec(memory_space=pltpu.VMEM)
    return pl.pallas_call(
        kernel,
        out_shape=(block, block),
        in_specs=[pl.BlockSpec(memory_space=pltpu.HBM)] * 3,
        out_specs=(whole, whole),
        scratch_shapes=scratch,
        compiler_params=pltpu.CompilerParams(
            collective_id=0, has_side_effects=True, vmem_limit_bytes=48 * 1024 * 1024
        ),
    )(source, conductance, pressure_start)


def solution(mesh):
    placed = (P("gx", "gy", "gz"), P("gx", "gy", "gz"), P("gx", "gy", "gz"))
    return jax.shard_map(
        per_device,
        mesh=mesh,
        in_specs=placed,
        out_specs=(P("gx", "gy", "gz"), P("gx", "gy", "gz")),
        check_vma=False,
    )
```

```python
import functools
import jax
import jax.numpy as jnp
from jax import lax
from jax.experimental import pallas as pl
from jax.experimental.pallas import tpu as pltpu
from jax.sharding import PartitionSpec as P

DEG = 3
COARSE_ITERS = 12
SHIFT = 0.001
UPPER_BOUND = 2.0
SMOOTH_FLOOR = 0.5
COARSE_FLOOR = 0.05

MESH = pl.DeviceIdType.MESH
AXES = ("gx", "gy", "gz")
COUNT = (4, 8, 8)
F32 = jnp.float32
SIGN = (1, -1)

NEAR = [
    (a, b, c)
    for c in (-1, 0, 1)
    for a in (-1, 0, 1)
    for b in (-1, 0, 1)
    if (a, b, c) != (0, 0, 0)
]
NEAR.sort(key=lambda o: -sum(map(abs, o)))
PLANE = [(a, b, 0) for a in range(4) for b in range(8) if (a, b) != (0, 0)]
RING = [(0, 0, c) for c in range(1, 8)]


def hops(offset):
    x, y, z = (min(s % n, n - s % n) for s, n in zip(offset, COUNT))
    return x + (y + 1) // 2 + z


PLANE.sort(key=lambda o: -hops(o))
RING.sort(key=lambda o: -hops(o))

def chebyshev_weights(number, floor_value):
    centre = 0.5 * (UPPER_BOUND + floor_value)
    half_width = 0.5 * (UPPER_BOUND - floor_value)
    ratio = centre / half_width
    factor = 1.0 / ratio
    weights = [(0.0, 1.0 / centre)]
    for _ in range(1, number):
        factor_next = 1.0 / (2.0 * ratio - factor)
        weights.append((factor_next * factor, 2.0 * factor_next / half_width))
        factor = factor_next
    return weights


def peer(offset):
    return tuple(
        lax.rem(lax.axis_index(axis) + (step + count), count)
        for axis, step, count in zip(AXES, offset, COUNT)
    )


def iota(shape, dim):
    return lax.broadcasted_iota(jnp.int32, shape, dim)


def roll(value, shift, dim):
    size = value.shape[dim]
    return pltpu.roll(value, shift % size, dim)


def parts_of(value):
    first = value.astype(jnp.bfloat16).astype(F32)
    rest = value - first
    second = rest.astype(jnp.bfloat16).astype(F32)
    return first, second, rest - second


def dot(value, matrix):
    rows = value.shape[0]
    out = jnp.dot(jnp.concatenate(parts_of(value), axis=0), matrix, preferred_element_type=F32)
    return (out[2 * rows :] + out[rows : 2 * rows]) + out[:rows]


def dot_rows(matrix, value):
    columns = value.shape[1]
    out = jnp.dot(matrix, jnp.concatenate(parts_of(value), axis=1), preferred_element_type=F32)
    return (out[:, 2 * columns :] + out[:, columns : 2 * columns]) + out[:, :columns]


def ones_where(mask, scale=1.0):
    return jnp.where(mask, F32(scale), F32(0.0))


def send(src, dst, ssem, rsem, offset):
    pltpu.make_async_remote_copy(
        src_ref=src, dst_ref=dst, send_sem=ssem, recv_sem=rsem,
        device_id=peer(offset), device_id_type=MESH,
    ).start()


def wait_bytes(ref, sem):
    pltpu.make_async_copy(ref, ref, sem).wait()


def pack_fine(ext, count, py, pz, pw):
    sub = iota((8, 128), 0)
    lane = iota((8, 128), 1)
    for a in range(count):
        for group in range(4):
            for r in range(2):
                first = 4 + 4 * group + r
                slot = 2 * group + r
                py[0, a, slot] = jnp.where(
                    sub >= 4, ext[a, first, 8:16, 0:128], roll(ext[a, first + 2, 8:16, 0:128], 4, 0)
                )
                py[1, a, slot] = jnp.where(
                    sub < 4, ext[a, first, 0:8, 0:128], roll(ext[a, first + 2, 0:8, 0:128], 4, 0)
                )
        for tile in range(2):
            acc = jnp.zeros((8, 128), F32)
            for x in range(16):
                row = ext[a, 4 + x, 8 * tile : 8 * tile + 8, 0:128]
                acc = jnp.where(lane // 8 == x, roll(row, 8 * x + 4, 1), acc)
            pz[a, tile] = acc
    for side in range(2):
        acc = jnp.zeros((8, 128), F32)
        for a in range(count):
            for tile in range(2):
                at = 2 * a + tile
                acc = jnp.where(
                    lane // 32 == at, roll(pz[a, tile], 32 * at - (0 if side else 96), 1), acc
                )
        pw[side] = acc


def send_fine(ext, py, pz, pw, recv, ssem, rsem):
    ry, rz, rxy, rxz, ryz, rxyz = recv
    for offset in NEAR:
        dx, dy, dz = offset
        xi, yi, zi = (0 if d == 1 else 1 for d in offset)
        kind = (dx != 0, dy != 0, dz != 0)
        tile = 1 if dy == 1 else 0
        planes = pl.ds(6, 2) if dx == 1 else pl.ds(0, 2)
        if kind == (True, False, False):
            src = ext.at[:, pl.ds(16 if dx == 1 else 4, 4), pl.ds(0, 16), pl.ds(0, 128)]
            dst = ext.at[:, pl.ds(0 if dx == 1 else 20, 4), pl.ds(0, 16), pl.ds(0, 128)]
            which = 0
        elif kind == (False, True, False):
            src, dst, which = py.at[yi], ry.at[yi], 1
        elif kind == (False, False, True):
            src, dst, which = pz, rz.at[zi], 2
        elif kind == (True, True, False):
            src, dst, which = py.at[yi, :, planes], rxy.at[xi, yi], 3
        elif kind == (True, False, True):
            src, dst, which = pw.at[xi], rxz.at[xi, zi], 4
        elif kind == (False, True, True):
            src, dst, which = pz.at[:, tile], ryz.at[yi, zi], 5
        else:
            src, dst, which = pw.at[xi], rxyz.at[xi, yi, zi], 6
        send(src, dst, ssem.at[which], rsem.at[which], offset)


def wait_fine(py, recv, sem):
    refs = (recv[0].at[:, :, pl.ds(0, 8)],) + recv
    for which in range(7):
        wait_bytes(refs[which], sem.at[which])


def unpack_fine(ext, count, recv):
    ry, rz, rxy, rxz, ryz, rxyz = recv
    sub = iota((8, 128), 0)
    lane = iota((8, 128), 1)
    low = sub < 4
    zleft = lane % 8 < 4

    def place(a, first, left, right):
        ext[a, first, 16:24, 0:128] = jnp.where(low, right, left)
        ext[a, first + 2, 16:24, 0:128] = roll(jnp.where(low, left, right), 4, 0)

    for a in range(count):
        for group in range(4):
            for r in range(2):
                slot = 2 * group + r
                place(a, 4 + 4 * group + r, ry[0, a, slot], ry[1, a, slot])
        for r in range(2):
            place(a, r, rxy[0, 0, a, r], rxy[0, 1, a, r])
            place(a, 20 + r, rxy[1, 0, a, r], rxy[1, 1, a, r])
        for tile in range(3):
            both = []
            for zi in range(2):
                if tile < 2:
                    both.append(rz[zi, a, tile])
                else:
                    both.append(jnp.where(low, ryz[1, zi, a], ryz[0, zi, a]))
            comb = jnp.where(zleft, both[0], both[1])
            for x in range(16):
                ext[a, 4 + x, 8 * tile : 8 * tile + 8, 128:256] = roll(comb, -(8 * x + 4), 1)
    for side in range(2):
        edge = jnp.where(zleft, rxz[side, 0], rxz[side, 1])
        left = jnp.where(zleft, rxyz[side, 0, 0], rxyz[side, 0, 1])
        right = jnp.where(zleft, rxyz[side, 1, 0], rxyz[side, 1, 1])
        corner = jnp.where(low, right, roll(left, -32, 1))
        for a in range(count):
            for tile in range(3):
                for n in range(4):
                    value = roll(corner, -(64 * a + 8 * n + 4), 1) if tile == 2 else roll(
                        edge, -(32 * (2 * a + tile) + 8 * n + 4), 1
                    )
                    ext[a, 20 * side + n, 8 * tile : 8 * tile + 8, 128:256] = value


def planes_loop(first, last, body):
    for x in range(first, last):
        body(x)


def make_coefficients(load, coef, diag, inverse, x):
    k = load(x)
    faces = [0.5 * (k + load(x + 1)), 0.5 * (k + load(x - 1))]
    yp = 0.5 * (k + roll(k, -1, 0))
    zp = 0.5 * (k + roll(k, -1, 1))
    faces += [yp, roll(yp, 1, 0), zp, roll(zp, 1, 1)]
    d = SHIFT + ((faces[0] + faces[1]) + (faces[2] + faces[3]) + (faces[4] + faces[5]))
    inv = 1.0 / d
    for n in range(6):
        coef[n, x] = faces[n] * inv
    diag[x] = d
    inverse[x] = inv
    return inv


def scaled_residual(load, coef, scaled, x):
    v = load(x)
    total = scaled[x] - v
    total = total + (coef[0, x] * load(x + 1) + coef[1, x] * load(x - 1))
    total = total + (coef[2, x] * roll(v, -1, 0) + coef[3, x] * roll(v, 1, 0))
    total = total + (coef[4, x] * roll(v, -1, 1) + coef[5, x] * roll(v, 1, 1))
    return v, total


def shifts_plane(ref, ix):
    sub = iota((8, 8, 128), 1)
    lane = iota((8, 8, 128), 2)
    cur = ref[ix]
    nxt = jnp.concatenate([cur[1:], cur[:1]], axis=0)
    prv = jnp.concatenate([cur[7:], cur[:7]], axis=0)
    yp = jnp.where(sub % 4 == 3, roll(nxt, 3, 1), roll(cur, -1, 1))
    ym = jnp.where(sub % 4 == 0, roll(prv, -3, 1), roll(cur, 1, 1))
    half = roll(cur, 4, 1)
    swap = roll(half, 64, 2)
    swap_next = roll(roll(ref[(ix + 1) % 4], 4, 1), 64, 2)
    swap_prev = roll(roll(ref[(ix + 3) % 4], 4, 1), 64, 2)
    xp = jnp.where(sub < 4, half, jnp.where(lane < 64, swap, swap_next))
    xm = jnp.where(sub >= 4, half, jnp.where(lane >= 64, swap, swap_prev))
    return cur, (xp, xm, yp, ym, roll(cur, -1, 2), roll(cur, 1, 2))


def kernel(
    source, conductance, start, pressure, residual,
    m_fine, m_middle, m_coarse, m_plane, m_tile, m_spread,
    pwk, pw, pwv, ek, ea, ev, va, vb, w0, fi0, coef0, diag0, inv0, pyk, pzk, py, pz, pyv, pzv,
    ryk, rzk, rxyk, rxzk, ryzk, rxyzk,
    ry, rz, rxy, rxz, ryz, rxyz, ryv, rzv, rxyv, rxzv, ryzv, rxyzv,
    tk, tkz, zk, tf, tfz, zf, yf, yzf, nr, k1, v1a, v1b, w1, fi1, coef1, diag1, inv1,
    gk, gf, mk, mf, v2a, v2b, w2, coef2, diag2, inv2,
    ck, cf, k3, f3, v3a, v3b, w3, coef3,
    sem_in, semk_s, semk_r, sem_s, sem_r, semv_s, semv_r, sem1, semn,
):
    weights = chebyshev_weights(DEG, SMOOTH_FLOOR)
    coarse_weights = chebyshev_weights(COARSE_ITERS, COARSE_FLOOR)
    gx, gy, gz = (lax.axis_index(axis) for axis in AXES)
    recv = (ry, rz, rxy, rxz, ryz, rxyz)
    recv_k = (ryk, rzk, rxyk, rxzk, ryzk, rxyzk)
    recv_v = (ryv, rzv, rxyv, rxzv, ryzv, rxyzv)

    everyone = list(dict.fromkeys(
        [tuple(s % n for s, n in zip(o, COUNT)) for o in NEAR + RING + PLANE]
    ))
    barrier = pltpu.get_barrier_semaphore()
    for offset in everyone:
        pl.semaphore_signal(barrier, inc=1, device_id=peer(offset), device_id_type=MESH)

    own = (pl.ds(4, 16), pl.ds(0, 16), pl.ds(0, 128))
    inputs = [
        pltpu.make_async_copy(ref, to.at[own], sem_in.at[n])
        for n, (ref, to) in enumerate(
            ((conductance, ek.at[0]), (start, ea.at[0]), (source, ea.at[1]))
        )
    ]
    for copy in inputs:
        copy.start()

    def restrict_fine(load, scale):
        rows = [
            jnp.concatenate(
                [load(4 * p) + load(4 * p + 1), load(4 * p + 2) + load(4 * p + 3)], axis=1
            )
            for p in range(4)
        ]
        mid = dot(jnp.concatenate(rows, axis=0), m_fine[...])
        wide = jnp.concatenate([mid[16 * p : 16 * p + 16] for p in range(4)], axis=1)
        left = ones_where(iota((8, 16), 1) // 2 == iota((8, 16), 0))
        out = dot_rows(left, wide)
        return [scale * out[:, 128 * p : 128 * p + 128] for p in range(4)]

    lane = iota((8, 128), 1)
    sub = iota((8, 128), 0)
    near_z = lane % 64 < 32
    near_y = sub < 4

    def half_z(first, second, which):
        if which == 0:
            return jnp.where(near_z, roll(second, -32, 1), first)
        return jnp.where(near_z, first, roll(second, 32, 1))

    def half_y(first, second, which):
        if which == 0:
            return jnp.where(near_y, roll(second, 4, 0), first)
        return jnp.where(near_y, first, roll(second, 4, 0))

    def sides(left, right):
        return (
            jnp.where(near_z, right, left),
            jnp.where(near_z, roll(right, -32, 1), roll(left, 32, 1)),
        )

    def place(put, x, tile, own, side):
        put(x, tile, jnp.where(lane < 64, own, roll(side, 64, 1)))
        put(x + 1, tile, jnp.where(lane < 64, roll(own, 64, 1), side))

    def pack_halves(tiles, zpack):
        for which in range(2):
            for n in range(2):
                zpack[which, n] = half_z(tiles[4, 2 * n], tiles[4, 2 * n + 1], which)

    def send_tile(tiles, zpack, ztiles, at):
        for dx, dy, dz in NEAR:
            slot = 3 * (1 - dx) + (1 - dy)
            if dz == 0:
                send(tiles.at[4], tiles.at[slot], sem1.at[at], sem1.at[at + 1], (dx, dy, dz))
            else:
                zi = 0 if dz == 1 else 1
                send(
                    zpack.at[zi], ztiles.at[zi, slot], sem1.at[at + 2], sem1.at[at + 3], (dx, dy, dz)
                )

    def wait_tile(tiles, ztiles, at):
        wait_bytes(tiles.at[pl.ds(0, 8)], sem1.at[at])
        wait_bytes(ztiles, sem1.at[at + 2])

    def unpack_tile(tiles, ztiles, put):
        for i in range(3):
            for j in range(3):
                base = 3 * i + j
                for n in range(2):
                    both = sides(ztiles[0, base, n], ztiles[1, base, n])
                    for r in range(2):
                        q = 2 * n + r
                        place(put, 8 * i + 2 * q, j, tiles[base, q], both[r])

    def near_slots(kind, xi, yi, zi):
        if kind == (True, False, False):
            return 2 * xi, 2
        if kind == (False, True, False):
            return 4 + 2 * yi, 2
        if kind == (False, False, True):
            return 8 + 2 * zi, 2
        if kind == (True, True, False):
            return 12 + 2 * xi + yi, 1
        if kind == (True, False, True):
            return 16 + 2 * xi + zi, 1
        if kind == (False, True, True):
            return 20 + 2 * yi + zi, 1
        return 24 + 4 * xi + 2 * yi + zi, 1

    def pack_near():
        pack_halves(tf, zf)
        for which in range(2):
            for n in range(2):
                yf[which, n] = half_y(tf[4, 2 * n], tf[4, 2 * n + 1], which)
            for other in range(2):
                yzf[which, other] = half_z(yf[which, 0], yf[which, 1], other)

    def send_near():
        for offset in NEAR:
            dx, dy, dz = offset
            xi, yi, zi = (0 if d == 1 else 1 for d in offset)
            kind = (dx != 0, dy != 0, dz != 0)
            at, size = near_slots(kind, xi, yi, zi)
            far = 1 - xi
            if kind == (True, False, False):
                src = tf.at[4, pl.ds(2 * far, 2)]
            elif kind == (False, True, False):
                src = yf.at[yi]
            elif kind == (False, False, True):
                src = zf.at[zi]
            elif kind == (True, True, False):
                src = yf.at[yi, pl.ds(far, 1)]
            elif kind == (True, False, True):
                src = zf.at[zi, pl.ds(far, 1)]
            else:
                src = yzf.at[yi, pl.ds(zi, 1)]
            send(src, nr.at[pl.ds(at, size)], semn.at[0], semn.at[1], offset)

    def unpack_near(put):
        def get(kind, xi, yi, zi, n=0):
            return nr[near_slots(kind, xi, yi, zi)[0] + n]

        x_, y_, z_ = (True, False, False), (False, True, False), (False, False, True)
        xy_, xz_, yz_, all_ = (True, True, False), (True, False, True), (False, True, True), (True,) * 3
        for n in range(2):
            both = sides(get(z_, 0, 0, 0, n), get(z_, 0, 0, 1, n))
            for r in range(2):
                place(put, 8 + 4 * n + 2 * r, 1, tf[4, 2 * n + r], both[r])
        for xi in range(2):
            first = 4 if xi == 0 else 16
            both = sides(get(xz_, xi, 0, 0), get(xz_, xi, 0, 1))
            for r in range(2):
                place(put, first + 2 * r, 1, get(x_, xi, 0, 0, r), both[r])
        for yi in range(2):
            tile = 2 * yi
            both = sides(get(yz_, 0, yi, 0), get(yz_, 0, yi, 1))
            for n in range(2):
                own = get(y_, 0, yi, 0, n)
                place(put, 8 + 4 * n, tile, own, both[n])
                place(put, 10 + 4 * n, tile, roll(own, 4, 0), roll(both[n], 4, 0))
            for xi in range(2):
                first = 4 if xi == 0 else 16
                side = sides(get(all_, xi, yi, 0), get(all_, xi, yi, 1))[1 - xi]
                own = get(xy_, xi, yi, 0)
                place(put, first, tile, own, side)
                place(put, first + 2, tile, roll(own, 4, 0), roll(side, 4, 0))

    def restrict_middle(rows, scale):
        i, j = iota((16, 64), 0), iota((16, 64), 1)
        x = 2 * (i // 8) + (i % 8) // 4
        left = ones_where((j // 16 == x) & ((j % 8) // 2 == i % 4))
        mid = dot_rows(left, rows)
        return scale * dot(jnp.concatenate([mid[0:8], mid[8:16]], axis=1), m_middle[...])

    def send_plane(message, plane, pair):
        slot = gx * 8 + gy
        plane[slot] = message[...]
        for offset in PLANE:
            send(message, plane.at[slot], sem1.at[pair], sem1.at[pair + 1], offset)

    def restrict_plane(load, scale, message):
        i, j = iota((8, 32), 0), iota((8, 32), 1)
        left = ones_where((j // 8 == i // 2) & ((j % 4) // 2 == i % 2))
        for tile in range(2):
            wide = jnp.concatenate(
                [load(ix)[4 * tile : 4 * tile + 4].reshape(32, 128) for ix in range(4)], axis=1
            )
            message[tile] = scale * dot(dot_rows(left, wide), m_plane[...])

    def send_ring(message, ring, pair):
        ring[gz] = message[...]
        for offset in RING:
            send(message, ring.at[gz], sem1.at[pair], sem1.at[pair + 1], offset)

    def unpack_ring(ring, out):
        lane = iota((8, 128), 1)
        for x in range(8):
            for tile in range(2):
                acc = jnp.zeros((8, 128), F32)
                for z in range(8):
                    acc = jnp.where(lane // 16 == z, roll(ring[z, tile], 16 * (z - x), 1), acc)
                out[x, 8 * tile : 8 * tile + 8] = acc

    inputs[0].wait()
    pack_fine(ek, 1, pyk, pzk, pwk)
    pl.semaphore_wait(barrier, len(everyone))
    send_fine(ek, pyk, pzk, pwk, recv_k, semk_s, semk_r)
    inputs[1].wait()
    inputs[2].wait()
    pack_fine(ea, 2, py, pz, pw)
    send_fine(ea, py, pz, pw, recv, sem_s, sem_r)

    i, j = iota((256, 128), 0), iota((256, 128), 1)
    m_fine[...] = ones_where((i // 128 == j // 64) & ((i % 128) // 2 == j % 64), 0.125)
    m_middle[...] = ones_where(
        (i // 128 == j // 64) & ((16 + (i % 128) // 2) % 64 == j % 64), 0.125
    )
    z = lax.rem(16 * gz + 120 + (j % 64) // 2, 128)
    m_coarse[...] = ones_where((i // 128 == j // 64) & (i % 128 == z))
    i, j = iota((512, 128), 0), iota((512, 128), 1)
    z = i % 64
    m_plane[...] = ones_where(
        (i // 64 == j // 16) & (z >= 16) & (z < 48) & ((z - 16) // 2 == j % 16), 0.125
    )
    i, j = iota((128, 256), 0), iota((128, 256), 1)
    m_tile[...] = ones_where((i // 64 == j // 128) & (i % 64 == (16 + (j % 128) // 2) % 64))
    m_spread[...] = ones_where(i == j // 2)
    for p, block in enumerate(restrict_fine(lambda x: ek[0, 4 + x, 0:16, 0:128], 0.25)):
        tk[4, p] = block
    pack_halves(tk, zk)
    wait_fine(pyk, recv_k, semk_r)
    unpack_fine(ek, 1, recv_k)
    planes_loop(1, 23, lambda x: make_coefficients(lambda i: ek[0, i], coef0, diag0, inv0, x))
    send_tile(tk, zk, tkz, 0)
    wait_fine(py, recv, sem_r)
    unpack_fine(ea, 2, recv)

    def fine_scale(x):
        fi0[x] = ea[1, x] * inv0[x]

    planes_loop(1, 23, fine_scale)

    def fine_sweep(load, out, index, first, last):
        carry, weight = weights[index]

        def body(x):
            v, r = scaled_residual(load, coef0, fi0, x)
            change = weight * r if index == 0 else carry * w0[x] + weight * r
            reach = 3 - index - max(4 - x, x - 19, 0)
            cuts = [(slice(0, 16), slice(0, 128))]
            if reach > 0:
                cuts += [(slice(16, 24), slice(0, 128)), (slice(0, 16), slice(128, 256))]
            if reach > 1:
                cuts += [(slice(16, 24), slice(128, 256))]
            for cut in cuts:
                if index < 2:
                    w0[(x,) + cut] = change[cut]
                out[(x,) + cut] = (v + change)[cut]

        planes_loop(first, last, body)

    fine_sweep(lambda i: ea[0, i], va, 0, 1, 23)
    fine_sweep(lambda i: va[i], vb, 1, 2, 22)
    fine_sweep(lambda i: vb[i], va, 2, 3, 21)

    def fine_residual(x):
        v, r = scaled_residual(lambda i: va[i], coef0, fi0, x)
        vb[x] = r * diag0[x]
        ev[0, x, 0:16, 0:128] = v[0:16, 0:128]

    planes_loop(4, 20, fine_residual)
    for p, block in enumerate(restrict_fine(lambda x: vb[4 + x, 0:16, 0:128], 1.0)):
        tf[4, p] = block
    pack_near()
    send_near()

    wait_tile(tk, tkz, 1)

    def put_k1(x, tile, value):
        k1[x, 8 * tile : 8 * tile + 8] = value

    unpack_tile(tk, tkz, put_k1)
    mk[...] = restrict_middle(k1[8:16, 8:16].reshape(64, 128), 0.25)
    send_plane(mk, gk, 8)
    planes_loop(1, 23, lambda x: make_coefficients(lambda i: k1[i], coef1, diag1, inv1, x))

    wait_bytes(nr, semn.at[1])

    def put_f1(x, tile, value):
        fi1[x, 8 * tile : 8 * tile + 8] = value

    unpack_near(put_f1)

    def middle_first(x):
        scaled = fi1[x] * inv1[x]
        fi1[x] = scaled
        change = weights[0][1] * scaled
        w1[x] = change
        v1a[x] = change

    def middle_sweep(load, out, index, first, last):
        carry, weight = weights[index]

        def body(x):
            v, r = scaled_residual(load, coef1, fi1, x)
            change = weight * r if index == 0 else carry * w1[x] + weight * r
            w1[x] = change
            out[x] = v + change

        planes_loop(first, last, body)

    def middle_before(first, last):
        planes_loop(first, last, middle_first)
        middle_sweep(lambda i: v1a[i], v1b, 1, first + 1, last - 1)
        middle_sweep(lambda i: v1b[i], v1a, 2, first + 2, last - 2)

    middle_before(5, 19)

    def middle_residual(x):
        _, r = scaled_residual(lambda i: v1a[i], coef1, fi1, x)
        v1b[x] = r * diag1[x]

    planes_loop(8, 16, middle_residual)
    mf[...] = restrict_middle(v1b[8:16, 8:16].reshape(64, 128), 1.0)
    send_plane(mf, gf, 12)
    send_tile(tf, zf, tfz, 4)

    wait_bytes(gk.at[pl.ds(0, 31)], sem1.at[9])
    k2 = gk.reshape(4, 8, 8, 128)
    f2 = gf.reshape(4, 8, 8, 128)
    restrict_plane(lambda ix: k2[ix], 0.25, ck.at[8])
    send_ring(ck.at[8], ck, 10)
    for ix in range(4):
        k, around = shifts_plane(k2, ix)
        faces = [0.5 * (k + other) for other in around]
        d = SHIFT + ((faces[0] + faces[1]) + (faces[2] + faces[3]) + (faces[4] + faces[5]))
        inv = 1.0 / d
        for n in range(6):
            coef2[n, ix] = faces[n] * inv
        diag2[ix] = d
        inv2[ix] = inv

    wait_bytes(gf.at[pl.ds(0, 31)], sem1.at[13])
    for ix in range(4):
        change = weights[0][1] * (f2[ix] * inv2[ix])
        w2[ix] = change
        v2a[ix] = change

    def plane_residual(ref, ix):
        v, around = shifts_plane(ref, ix)
        total = f2[ix] * inv2[ix] - v
        for n in range(6):
            total = total + coef2[n, ix] * around[n]
        return v, total

    def plane_sweep(ref, out, index):
        carry, weight = weights[index]
        for ix in range(4):
            v, r = plane_residual(ref, ix)
            change = weight * r if index == 0 else carry * w2[ix] + weight * r
            w2[ix] = change
            out[ix] = v + change

    plane_sweep(v2a, v2b, 1)
    plane_sweep(v2b, v2a, 2)
    for ix in range(4):
        v2b[ix] = plane_residual(v2a, ix)[1] * diag2[ix]
    restrict_plane(lambda ix: v2b[ix], 1.0, cf.at[8])
    send_ring(cf.at[8], cf, 14)

    pack_fine(ev, 1, pyv, pzv, pwv)
    send_fine(ev, pyv, pzv, pwv, recv_v, semv_s, semv_r)
    wait_tile(tf, tfz, 5)
    unpack_tile(tf, tfz, put_f1)
    middle_before(1, 23)

    wait_bytes(ck.at[pl.ds(0, 7)], sem1.at[11])
    unpack_ring(ck, k3)
    for x in range(8):
        k = k3[x]
        faces = [0.5 * (k + k3[(x + 1) % 8]), 0.5 * (k + k3[(x + 7) % 8])]
        faces += [0.5 * (k + roll(k, s, dim)) for dim in (0, 1) for s in (-1, 1)]
        d = SHIFT + ((faces[0] + faces[1]) + (faces[2] + faces[3]) + (faces[4] + faces[5]))
        inv = 1.0 / d
        for n in range(6):
            coef3[n, x] = faces[n] * inv
        coef3[6, x] = inv
    wait_bytes(cf.at[pl.ds(0, 7)], sem1.at[15])
    unpack_ring(cf, f3)
    for x in range(8):
        scaled = f3[x] * coef3[6, x]
        f3[x] = scaled
        change = coarse_weights[0][1] * scaled
        w3[x] = change
        v3a[x] = change
    bufs = (v3a, v3b)
    for index in range(1, COARSE_ITERS):
        old, new = bufs[(index + 1) % 2], bufs[index % 2]
        carry, weight = coarse_weights[index]
        for x in range(8):
            v = old[x]
            total = f3[x] - v
            total = total + (coef3[0, x] * old[(x + 1) % 8] + coef3[1, x] * old[(x + 7) % 8])
            total = total + (coef3[2, x] * roll(v, -1, 0) + coef3[3, x] * roll(v, 1, 0))
            total = total + (coef3[4, x] * roll(v, -1, 1) + coef3[5, x] * roll(v, 1, 1))
            change = carry * w3[x] + weight * total
            w3[x] = change
            new[x] = v + change
    v3 = bufs[(COARSE_ITERS - 1) % 2]

    rows = jnp.concatenate(
        [jnp.concatenate([v3[2 * ix], v3[2 * ix + 1]], axis=1) for ix in range(4)], axis=0
    )
    mid = dot(rows, m_coarse[...])
    wide = jnp.concatenate([mid[16 * ix : 16 * ix + 16] for ix in range(4)], axis=1)
    i, j = iota((64, 16), 0), iota((64, 16), 1)
    left = ones_where(j == 2 * (i // 8) + (i % 4) // 2)
    spread = dot_rows(left, wide)
    for ix in range(4):
        v2b[ix] = v2a[ix] + spread[:, 128 * ix : 128 * ix + 128].reshape(8, 8, 128)
    plane_sweep(v2b, v2a, 0)
    plane_sweep(v2a, v2b, 1)
    plane_sweep(v2b, v2a, 2)

    tiles = [
        v2a[lax.rem(gx + i + 3, 4), lax.rem(gy + j + 7, 8)] for i in range(3) for j in range(3)
    ]
    mid = dot(jnp.concatenate(tiles, axis=0), m_tile[...])
    wide = jnp.concatenate([mid[8 * t : 8 * t + 8] for t in range(9)], axis=1)
    i, j = iota((32, 8), 0), iota((32, 8), 1)
    left = ones_where(j == (i // 16) * 4 + (i % 8) // 2)
    spread = dot_rows(left, wide)
    for t in range(9):
        for h in range(2):
            for x in range(4):
                plane = 8 * (t // 3) + 4 * h + x
                at = 8 * (t % 3)
                v1b[plane, at : at + 8] = (
                    v1a[plane, at : at + 8]
                    + spread[8 * x : 8 * x + 8, 256 * t + 128 * h : 256 * t + 128 * h + 128]
                )
    middle_sweep(lambda i: v1b[i], v1a, 0, 4, 20)
    middle_sweep(lambda i: v1a[i], v1b, 1, 5, 19)
    middle_sweep(lambda i: v1b[i], v1a, 2, 6, 18)

    wait_fine(pyv, recv_v, semv_r)
    unpack_fine(ev, 1, recv_v)
    wide = jnp.concatenate([v1a[6 + p] for p in range(12)], axis=1)
    i, j = iota((24, 24), 0), iota((24, 24), 1)
    left = ones_where(j == jnp.where(i < 20, 8 + i // 2, i // 2 - 4))
    mid = dot_rows(left, wide)
    spread = dot(
        jnp.concatenate([mid[:, 128 * p : 128 * p + 128] for p in range(12)], axis=0), m_spread[...]
    )
    for p in range(12):
        for u in range(2):
            va[2 * p + u] = ev[0, 2 * p + u] + spread[24 * p : 24 * p + 24]
    fine_sweep(lambda i: va[i], vb, 0, 1, 23)
    fine_sweep(lambda i: vb[i], va, 1, 2, 22)
    fine_sweep(lambda i: va[i], vb, 2, 3, 21)

    def fine_last(x):
        v, r = scaled_residual(lambda i: vb[i], coef0, fi0, x)
        pressure[x - 4] = v[0:16, 0:128]
        residual[x - 4] = (r * diag0[x])[0:16, 0:128]

    planes_loop(4, 20, fine_last)

    wait_fine(pyk, recv_k, semk_s)
    wait_fine(py, recv, sem_s)
    wait_fine(pyv, recv_v, semv_s)
    wait_tile(tk, tkz, 0)
    wait_bytes(nr, semn.at[0])
    wait_tile(tf, tfz, 4)
    wait_bytes(gk.at[pl.ds(0, 31)], sem1.at[8])
    wait_bytes(ck.at[pl.ds(0, 7)], sem1.at[10])
    wait_bytes(gf.at[pl.ds(0, 31)], sem1.at[12])
    wait_bytes(cf.at[pl.ds(0, 7)], sem1.at[14])


def vmem(*shape):
    return pltpu.VMEM(shape, F32)


def fine_buffers(count):
    return [
        vmem(2, count, 8, 8, 128), vmem(2, count, 2, 8, 128), vmem(2, 2, count, 2, 8, 128),
        vmem(2, 2, 8, 128), vmem(2, 2, count, 8, 128), vmem(2, 2, 2, 8, 128),
    ]


def per_device(source, conductance, pressure_start):
    fine = (24, 24, 256)
    middle = (24, 24, 128)
    plane = (4, 8, 8, 128)
    coarse = (8, 16, 128)
    scratch = [
        vmem(256, 128), vmem(256, 128), vmem(256, 128), vmem(512, 128), vmem(128, 256), vmem(128, 256),
        vmem(2, 8, 128), vmem(2, 8, 128), vmem(2, 8, 128),
        vmem(1, *fine), vmem(2, *fine), vmem(1, *fine), vmem(*fine), vmem(*fine), vmem(*fine), vmem(*fine),
        vmem(6, *fine), vmem(*fine), vmem(*fine),
        vmem(2, 1, 8, 8, 128), vmem(1, 2, 8, 128), vmem(2, 2, 8, 8, 128), vmem(2, 2, 8, 128), vmem(2, 1, 8, 8, 128), vmem(1, 2, 8, 128),
    ]
    scratch += fine_buffers(1) + fine_buffers(2) + fine_buffers(1)
    scratch += [
        vmem(9, 4, 8, 128), vmem(2, 9, 2, 8, 128), vmem(2, 2, 8, 128),
        vmem(9, 4, 8, 128), vmem(2, 9, 2, 8, 128), vmem(2, 2, 8, 128),
        vmem(2, 2, 8, 128), vmem(2, 2, 8, 128), vmem(32, 8, 128), vmem(*middle), vmem(*middle), vmem(*middle),
        vmem(*middle), vmem(*middle), vmem(6, *middle), vmem(*middle), vmem(*middle),
        vmem(32, 8, 128), vmem(32, 8, 128), vmem(8, 128), vmem(8, 128),
        vmem(*plane), vmem(*plane), vmem(*plane), vmem(6, *plane), vmem(*plane), vmem(*plane),
        vmem(9, 2, 8, 128), vmem(9, 2, 8, 128), vmem(*coarse), vmem(*coarse), vmem(*coarse),
        vmem(*coarse), vmem(*coarse), vmem(7, *coarse),
        pltpu.SemaphoreType.DMA((3,)),
        pltpu.SemaphoreType.DMA((7,)), pltpu.SemaphoreType.DMA((7,)),
        pltpu.SemaphoreType.DMA((7,)), pltpu.SemaphoreType.DMA((7,)),
        pltpu.SemaphoreType.DMA((7,)), pltpu.SemaphoreType.DMA((7,)),
        pltpu.SemaphoreType.DMA((16,)), pltpu.SemaphoreType.DMA((2,)),
    ]
    block = jax.ShapeDtypeStruct(source.shape, F32)
    whole = pl.BlockSpec(memory_space=pltpu.VMEM)
    return pl.pallas_call(
        kernel,
        out_shape=(block, block),
        in_specs=[pl.BlockSpec(memory_space=pltpu.HBM)] * 3,
        out_specs=(whole, whole),
        scratch_shapes=scratch,
        compiler_params=pltpu.CompilerParams(
            collective_id=0, has_side_effects=True, vmem_limit_bytes=48 * 1024 * 1024
        ),
    )(source, conductance, pressure_start)


def solution(mesh):
    placed = (P("gx", "gy", "gz"), P("gx", "gy", "gz"), P("gx", "gy", "gz"))
    return jax.shard_map(
        per_device,
        mesh=mesh,
        in_specs=placed,
        out_specs=(P("gx", "gy", "gz"), P("gx", "gy", "gz")),
        check_vma=False,
    )
```
